512 devices in a mesh: lon: 32 (over y, x, core), lat: 16 (over z).
Axes of the slice: x: 4, y: 4, z: 16, core: 2. Of those that a mesh axis runs over, the one named last changes fastest.
Arguments:
- direction: float32 [75, 128, 4096], P(None, 'lat', 'lon'), may hold values from -40 to 40
- residual: float32 [75, 128, 4096], P(None, 'lat', 'lon'), may hold values from -40 to 40
- eof_basis: float32 [75, 75], replicated, may hold values from -0.75 to 0.75
- kappa_east: float32 [128, 4096], P('lat', 'lon'), may hold values from 0.02 to 0.24
- kappa_north: float32 [128, 4096], P('lat', 'lon'), may hold values from 0.02 to 0.24
- wet_mask: int32 [128, 4096], P('lat', 'lon'), may hold values 0 or 1
- obs_base: int32 [16, 32, 256], P('lat', 'lon'), may hold values from 0 to 1023, as said below
- obs_frac: float32 [2, 16, 32, 256], P(None, 'lat', 'lon'), may hold values from 0 to 1
- obs_rinv: float32 [75, 16, 32, 256], P(None, 'lat', 'lon'), may hold values from 0.25 to 4
Outputs:
- new_residual: float32 [75, 128, 4096], P(None, 'lat', 'lon')
- new_direction: float32 [75, 128, 4096], P(None, 'lat', 'lon')
- step_length: float32 [], replicated
The draws below stay inside these ranges and needn't reach their ends.
Inputs may be any that keep to these rules, and one draw needn't show every extreme that they name: `obs_base`: s // 128 and s % 128 are the row and column of the square's south-west cell within the tile; no profile of the top tile row has its south-west cell in the grid's top row.
All inputs are finite; a program needn't handle non-finite values. No bound on the sum of `wet_mask` on one device may be relied on, other than what follows from the above.
Results may differ from the reference program's by a relative error of at most 0.000066.
Values sent between devices are 32-bit elements; how exact they have to be, the bound alone decides.
No kernel may reach another device: no remote copies, remote signals or barrier semaphores. Data moves between devices by JAX's collectives and lax.ppermute only.
A program may use at most 64 MiB of HBM per device.

```python
import math
from functools import partial
import jax
import jax.numpy as jnp
from jax import lax

K = 75
CLAT = 8
CLON = 128
OBS_DEV = 256
NLAT = 128
NLON = 4096
N_LON = 32
N_LAT = 16


def scaled_field(key, stream_id):
    key_main = jax.random.fold_in(key, stream_id)
    key_a, key_b = jax.random.split(key_main)
    lat_pos = jnp.arange(NLAT, dtype=jnp.float32) / max(NLAT - 1, 1)
    lon_pos = jnp.arange(NLON, dtype=jnp.float32) / max(NLON - 1, 1)
    random_part = jax.random.truncated_normal(key_a, -4.0, 4.0, (K, NLAT, NLON), jnp.float32)
    trend_exp = 0.5 * (lat_pos[:, None] + lon_pos[None, :]) - 0.5
    level_scale = 10.0 ** (jax.random.uniform(key_b, (K,), jnp.float32) - 0.5)
    return random_part * level_scale[:, None, None] * (10.0 ** trend_exp)[None]


def draw_direction(key, part):
    return scaled_field(key, 11)


def draw_residual(key, part):
    return scaled_field(key, 23)


def draw_obs_base(key, part):
    key_row, key_col = jax.random.split(jax.random.fold_in(key, 7))
    tiles_lat = NLAT // CLAT
    tiles_lon = NLON // CLON
    out_shape = (tiles_lat, tiles_lon, OBS_DEV)
    top_tile = jnp.arange(tiles_lat, dtype=jnp.int32)[:, None, None] == tiles_lat - 1
    row_limit = jnp.broadcast_to(jnp.where(top_tile, CLAT - 1, CLAT), out_shape).astype(jnp.int32)
    rows_drawn = jax.random.randint(key_row, out_shape, 0, row_limit, dtype=jnp.int32)
    cols_drawn = jax.random.randint(key_col, out_shape, 0, CLON, dtype=jnp.int32)
    base_cells = rows_drawn * CLON + cols_drawn
    base_cells = base_cells.at[0, 0, 0].set(CLAT * CLON - 1)
    return base_cells.at[0, 0, 1].set(0)


def plant(drawn, own_key, low, largest):
    longest = drawn.shape.index(max(drawn.shape))
    spots = []
    for shift in (0, 1):
        where = [jax.random.randint(jax.random.fold_in(own_key, axis), (), 0, length) for axis, length in enumerate(drawn.shape)]
        where[longest] = (where[longest] + shift) % drawn.shape[longest]
        spots.append(tuple(where))
    return drawn.at[spots[0]].set(low).at[spots[1]].set(largest)


def shard_levels(own_key, dims, cuts, smallest, high):
    factor_of, own = 1.0, jax.random.fold_in(own_key, 6)
    for position, shards_of in cuts:
        draws = jnp.exp(jax.random.uniform(jax.random.fold_in(own, position), (shards_of,), jnp.float32, smallest / len(cuts), high / len(cuts)))
        factor_of = factor_of * jnp.repeat(draws, dims[position] // shards_of).reshape([-1 if axis == position else 1 for axis in range(len(dims))])
    return factor_of


def gaussian(own_key, dims, spread, reach, held_as=jnp.bfloat16):
    return jnp.clip(spread * jax.random.normal(own_key, dims, jnp.float32), -reach, reach).astype(held_as)


def setup_inputs(seed: int = 0) -> dict:
    streams_of = jax.random.split(jax.random.key(seed), 10)
    direction = draw_direction(jax.random.fold_in(streams_of[9], 71), 0)
    residual = draw_residual(jax.random.fold_in(streams_of[9], 71), 0)
    eof_basis = gaussian(streams_of[2], (K, K), K ** -0.5, 0.75, jnp.float32)
    kappa_east = jnp.clip(jnp.exp(math.log(0.24) - 2.4849066 * jax.random.uniform(streams_of[3], (NLAT, NLON), jnp.float32) ** shard_levels(streams_of[3], (NLAT, NLON), ((0, 16), (1, 32)), -0.2, 0.2)), 0.02, 0.24)
    kappa_north = jnp.clip(jnp.exp(math.log(0.24) - 2.4849066 * jax.random.uniform(streams_of[4], (NLAT, NLON), jnp.float32) ** shard_levels(streams_of[4], (NLAT, NLON), ((0, 16), (1, 32)), -0.2, 0.2)), 0.02, 0.24)
    wet_mask = plant((jax.random.randint(streams_of[5], (NLAT, NLON), 0, 5) < 4).astype(jnp.int32), jax.random.fold_in(streams_of[5], 1), 0, 1)
    obs_base = draw_obs_base(jax.random.fold_in(streams_of[9], 71), 0)
    obs_frac = jnp.clip(1.0 * jax.random.uniform(streams_of[7], (2, N_LAT, N_LON, OBS_DEV), jnp.float32) ** shard_levels(streams_of[7], (2, N_LAT, N_LON, OBS_DEV), ((1, 16), (2, 32)), -0.2, 0.2), 0.0, 1.0)
    obs_rinv = jnp.clip(jnp.exp(math.log(4.0) - 2.7725887 * jax.random.uniform(streams_of[8], (K, N_LAT, N_LON, OBS_DEV), jnp.float32) ** shard_levels(streams_of[8], (K, N_LAT, N_LON, OBS_DEV), ((1, 16), (2, 32)), -0.2, 0.2)), 0.25, 4.0)
    return dict(direction=direction, residual=residual, eof_basis=eof_basis, kappa_east=kappa_east, kappa_north=kappa_north, wet_mask=wet_mask, obs_base=obs_base, obs_frac=obs_frac, obs_rinv=obs_rinv)


def three_steps(plane, east_face, north_face, fold_face):
    west_face = jnp.roll(east_face, 1, axis=1)
    south_face = jnp.concatenate([jnp.zeros_like(north_face[:1]), north_face[:-1]], 0)
    for step_index in range(3):
        zero_line = jnp.zeros_like(plane[:1])
        north_vals = jnp.concatenate([plane[1:], zero_line], 0)
        south_vals = jnp.concatenate([zero_line, plane[:-1]], 0)
        change = east_face * (jnp.roll(plane, -1, axis=1) - plane)
        change = change + west_face * (jnp.roll(plane, 1, axis=1) - plane)
        change = change + north_face * (north_vals - plane) + south_face * (south_vals - plane)
        change = change.at[-1].add(fold_face * (plane[-1, ::-1] - plane[-1]))
        plane = plane + change
    return plane


def reference(direction, residual, eof_basis, kappa_east, kappa_north, wet_mask, obs_base, obs_frac, obs_rinv):
    wet_float = wet_mask.astype(jnp.float32)
    east_face = kappa_east * wet_float * jnp.roll(wet_float, -1, axis=1)
    wet_above = jnp.concatenate([wet_float[1:], jnp.zeros_like(wet_float[:1])], 0)
    north_face = kappa_north * wet_float * wet_above
    fold_face = 0.5 * (kappa_north[-1] + kappa_north[-1, ::-1]) * wet_float[-1] * wet_float[-1, ::-1]
    diffuse_all = partial(three_steps, east_face=east_face, north_face=north_face, fold_face=fold_face)

    control = direction.reshape(K, -1)
    physical = jnp.dot(eof_basis, control, precision=lax.Precision.HIGHEST, preferred_element_type=jnp.float32)
    physical = lax.map(diffuse_all, physical.reshape(K, NLAT, NLON))
    flat_field = physical.reshape(K, -1)

    row_in = obs_base // CLON
    col_in = obs_base % CLON
    tile_lat = jnp.arange(N_LAT, dtype=jnp.int32)[:, None, None]
    tile_lon = jnp.arange(N_LON, dtype=jnp.int32)[None, :, None]
    glob_row = (tile_lat * CLAT + row_in).reshape(-1)
    glob_col = (tile_lon * CLON + col_in).reshape(-1)
    next_col = (glob_col + 1) % NLON
    corner_index = (glob_row * NLON + glob_col, glob_row * NLON + next_col,
                    (glob_row + 1) * NLON + glob_col, (glob_row + 1) * NLON + next_col)
    lat_frac = obs_frac[0].reshape(-1)
    lon_frac = obs_frac[1].reshape(-1)
    corner_weight = ((1.0 - lat_frac) * (1.0 - lon_frac), (1.0 - lat_frac) * lon_frac,
                     lat_frac * (1.0 - lon_frac), lat_frac * lon_frac)
    profiles = jnp.zeros((K, lat_frac.shape[0]), jnp.float32)
    for corner in range(4):
        profiles = profiles + corner_weight[corner][None, :] * flat_field[:, corner_index[corner]]
    weighted = obs_rinv.reshape(K, -1) * profiles
    adjoint = jnp.zeros((K, NLAT * NLON), jnp.float32)
    for corner in range(4):
        adjoint = adjoint.at[:, corner_index[corner]].add(corner_weight[corner][None, :] * weighted)
    adjoint = lax.map(diffuse_all, adjoint.reshape(K, NLAT, NLON))
    back = jnp.dot(eof_basis.T, adjoint.reshape(K, -1), precision=lax.Precision.HIGHEST, preferred_element_type=jnp.float32)
    image = direction + back.reshape(K, NLAT, NLON)

    old_norm = jnp.sum(residual * residual)
    curvature = jnp.sum(direction * image)
    step_length = old_norm / curvature
    new_residual = residual - step_length * image
    new_norm = jnp.sum(new_residual * new_residual)
    new_direction = new_residual + (new_norm / old_norm) * direction
    return new_residual, new_direction, step_length
```

```python
import functools

import jax
import jax.numpy as jnp
from jax import lax
from jax.experimental import pallas as pl
from jax.experimental.pallas import tpu as pltpu
from jax.sharding import PartitionSpec as P

HIGHEST = lax.Precision.HIGHEST
LANES = 128
ROWS = 8
PAD = 80
BAND = 3 * ROWS
HALO = 7
SLOTS = 12
SOUTH, OWN, NORTH = 0, 1, 2

SMEM = pl.BlockSpec(memory_space=pltpu.SMEM)
VMEM = pl.BlockSpec(memory_space=pltpu.VMEM)


def split(x):
    high = x.astype(jnp.bfloat16)
    return high, (x - high.astype(jnp.float32)).astype(jnp.bfloat16)


def dot3(left, right, dims):
    (lh, ll), (rh, rl) = left, right
    mul = functools.partial(
        lax.dot_general, dimension_numbers=(dims, ((), ())), preferred_element_type=jnp.float32
    )
    return mul(lh, rh) + (mul(lh, rl) + mul(ll, rh))


def pack_tile(eof_ref, dir_ref, ke_ref, kn_ref, wet_ref, base_ref, frac_ref, rinv_ref, out_ref):
    levels = dir_ref.shape[0]
    zeros = jnp.zeros((PAD - levels - 3, LANES), jnp.float32)
    eof = eof_ref[...]
    for row in range(ROWS):
        out_ref[row, :levels, :] = jnp.dot(
            eof, dir_ref[:, row, :], precision=HIGHEST, preferred_element_type=jnp.float32
        )
        out_ref[row, levels : levels + 1, :] = ke_ref[row : row + 1, :]
        out_ref[row, levels + 1 : levels + 2, :] = kn_ref[row : row + 1, :]
        out_ref[row, levels + 2 : levels + 3, :] = wet_ref[row : row + 1, :].astype(jnp.float32)
        out_ref[row, levels + 3 :, :] = zeros
    for half in range(2):
        cut = slice(half * LANES, (half + 1) * LANES)
        out_ref[ROWS + half, :levels, :] = rinv_ref[:, cut]
        out_ref[ROWS + half, levels : levels + 1, :] = base_ref[:, cut].astype(jnp.float32)
        out_ref[ROWS + half, levels + 1 : levels + 3, :] = frac_ref[:, cut]
        out_ref[ROWS + half, levels + 3 :, :] = zeros


def pack_columns(flags, own_ref, ra_ref, rb_ref, ns_ref, pa_ref, pb_ref):
    lat_even, lon_even, is_top = flags[0] == 1, flags[1] == 1, flags[2] == 1

    @pl.when(lat_even)
    def _():
        ns_ref[0] = ra_ref[...]
        ns_ref[1] = rb_ref[...]

    @pl.when(jnp.logical_not(lat_even))
    def _():
        ns_ref[0] = rb_ref[...]
        ns_ref[1] = ra_ref[...]

    @pl.when(is_top)
    def _():
        first = lax.broadcasted_iota(jnp.int32, (LANES, LANES), 0)
        second = lax.broadcasted_iota(jnp.int32, (LANES, LANES), 1)
        flip = jnp.where(first + second == LANES - 1, 1.0, 0.0).astype(jnp.float32)
        for row in range(ROWS):
            ns_ref[0, row] = jnp.dot(
                rb_ref[ROWS - 1 - row], flip, precision=HIGHEST, preferred_element_type=jnp.float32
            )

    lane = lax.broadcasted_iota(jnp.int32, (8, LANES), 1)

    def one(step, _):
        cut = pl.ds(pl.multiple_of(step * 8, 8), 8)
        for group in range(2):
            west = jnp.zeros((8, LANES), jnp.float32)
            east = jnp.zeros((8, LANES), jnp.float32)
            for slot in range(SLOTS):
                index = group * SLOTS + slot
                if index < ROWS:
                    tile = ns_ref[1, index, cut, :]
                elif index < 2 * ROWS:
                    tile = own_ref[index - ROWS, cut, :]
                else:
                    tile = ns_ref[0, index - 2 * ROWS, cut, :]
                start = HALO * slot
                here = (lane >= start) & (lane < start + HALO)
                west = jnp.where(here, pltpu.roll(tile, start, 1) if start else tile, west)
                east = jnp.where(here, pltpu.roll(tile, (start + HALO) % LANES, 1), east)
            pa_ref[group, cut, :] = jnp.where(lon_even, east, west)
            pb_ref[group, cut, :] = jnp.where(lon_even, west, east)
        return 0

    lax.fori_loop(0, PAD // 8, one, 0)
    for half in range(2):
        for ref in (pa_ref, pb_ref):
            ref[2 + 2 * SOUTH + half] = ns_ref[1, ROWS + half]
            ref[2 + 2 * OWN + half] = own_ref[ROWS + half]
            ref[2 + 2 * NORTH + half] = ns_ref[0, ROWS + half]


def diffuse_row(src, dst, coef, index, cut):
    centre = src[index, cut, :]
    width = centre.shape[1]
    wide = lambda k: jnp.broadcast_to(coef[k, pl.ds(index, 1), :], centre.shape)
    out = centre * wide(0)
    out = out + wide(1) * pltpu.roll(centre, width - 1, 1)
    out = out + wide(2) * pltpu.roll(centre, 1, 1)
    out = out + wide(3) * src[index + 1, cut, :]
    out = out + wide(4) * src[index - 1, cut, :]
    dst[index, cut, :] = out


def diffuse_all(one, two, coef, low, high):
    def body(step, _):
        cut = pl.ds(pl.multiple_of(step * 8, 8), 8)
        for src, dst, trim in ((one, two, 0), (two, one, 1), (one, two, 2)):
            for index in range(low + trim, high - trim):
                diffuse_row(src, dst, coef, index, cut)
        return 0

    lax.fori_loop(0, PAD // 8, body, 0)


def local_image(
    flags,
    own_ref,
    ns_ref,
    qa_ref,
    qb_ref,
    dir_ref,
    res_ref,
    eoft_ref,
    img_ref,
    part_ref,
    field,
    other,
    adj,
    coef,
    obs,
):
    lon_even, is_top = flags[1] == 1, flags[2] == 1
    levels = dir_ref.shape[0]
    width = 2 * LANES
    lane = lax.broadcasted_iota(jnp.int32, (8, LANES), 1)

    def unpack(step, _):
        cut = pl.ds(pl.multiple_of(step * 8, 8), 8)
        for group in range(2):
            first, second = qa_ref[group, cut, :], qb_ref[group, cut, :]
            east = jnp.where(lon_even, first, second)
            west = jnp.where(lon_even, second, first)
            for slot in range(SLOTS):
                index = group * SLOTS + slot
                if index < ROWS:
                    tile = ns_ref[1, index, cut, :]
                elif index < 2 * ROWS:
                    tile = own_ref[index - ROWS, cut, :]
                else:
                    tile = ns_ref[0, index - 2 * ROWS, cut, :]
                start = HALO * slot
                from_east = pltpu.roll(east, (LANES - start) % LANES, 1) if start else east
                from_west = pltpu.roll(west, (LANES - HALO - start) % LANES, 1)
                halo = jnp.where(
                    lane < HALO, from_east, jnp.where(lane >= LANES - HALO, from_west, 0.0)
                )
                field[index, cut, :LANES] = tile
                field[index, cut, LANES:] = halo
        return 0

    lax.fori_loop(0, PAD // 8, unpack, 0)

    ke, kn, wet = field[:, levels, :], field[:, levels + 1, :], field[:, levels + 2, :]
    row = lax.broadcasted_iota(jnp.int32, (BAND, width), 0)
    up = lambda x: jnp.concatenate([x[1:], x[:1]], 0)
    down = lambda x: jnp.concatenate([x[-1:], x[:-1]], 0)
    right = lambda x: pltpu.roll(x, width - 1, 1)
    left = lambda x: pltpu.roll(x, 1, 1)
    seam = 2 * ROWS - 1
    top = jnp.where(is_top, 1, 0)
    ke = jnp.where((row > seam) & (top == 1), right(ke), ke)
    kn_up = up(kn)
    kn = jnp.where(
        top == 1, jnp.where(row > seam, kn_up, jnp.where(row == seam, 0.5 * (kn + kn_up), kn)), kn
    )
    east_face = ke * wet * right(wet)
    north_face = kn * wet * up(wet)
    west_face, south_face = left(east_face), down(north_face)
    coef[0] = 1.0 - east_face - west_face - north_face - south_face
    coef[1] = east_face
    coef[2] = west_face
    coef[3] = north_face
    coef[4] = south_face

    diffuse_all(field, other, coef, 2, BAND - 2)
    physical = other

    keep = lax.broadcasted_iota(jnp.int32, (PAD, LANES), 0) < levels
    for band in range(3):
        for half in range(2):
            cut = slice(half * LANES, (half + 1) * LANES)
            slot = 2 + 2 * band + half
            first, second = qa_ref[slot], qb_ref[slot]
            mid = (ns_ref[1, ROWS + half], own_ref[ROWS + half], ns_ref[0, ROWS + half])[band]
            obs[0, band, :, cut] = jnp.where(lon_even, second, first)
            obs[1, band, :, cut] = mid
            obs[2, band, :, cut] = jnp.where(lon_even, first, second)
    adj[...] = jnp.zeros(adj.shape, jnp.float32)
    cells = lax.broadcasted_iota(jnp.int32, (width, width), 0)
    keep = lax.broadcasted_iota(jnp.int32, (PAD, width), 0) < levels
    spans = ((4, 9, 5), (8, 17, 8), (16, 20, 16))
    ends = (9, 17, 19)
    for band in range(3):
        begin, stop, adj_begin = spans[band]
        adj_stop = ends[band]
        lhs = split(physical[begin:stop].reshape((stop - begin) * PAD, width))

        def tile_of(t, _, band=band, lhs=lhs, begin=begin, stop=stop, lo=adj_begin, hi=adj_stop):
            base = obs[t, band, levels : levels + 1, :].astype(jnp.int32)
            p = obs[t, band, levels + 1 : levels + 2, :]
            q = obs[t, band, levels + 2 : levels + 3, :]
            j, i = base >> 7, base & (LANES - 1)
            rows, cols = j + ROWS * band, i
            a0, a1, b0, b1 = 1.0 - p, p, 1.0 - q, q
            if band == NORTH:
                turned = top == 1
                rows = jnp.where(turned, 22 - j, rows)
                cols = jnp.where(turned, 126 - i, cols)
                a0, a1 = jnp.where(turned, a1, a0), jnp.where(turned, a0, a1)
                b0, b1 = jnp.where(turned, b1, b0), jnp.where(turned, b0, b1)
            near = jnp.where(t == 1, 1, jnp.where(t == 0, jnp.where(cols >= 64, 1, 0), jnp.where(cols < 64, 1, 0)))
            b0, b1 = jnp.where(near == 1, b0, 0.0), jnp.where(near == 1, b1, 0.0)
            lane0 = (cols + jnp.where(t == 1, 0, LANES)) & (width - 1)
            lane1 = (lane0 + 1) & (width - 1)
            weight = jnp.where(cells == lane0, b0, jnp.where(cells == lane1, b1, 0.0))
            rhs = split(weight)
            taken = dot3(lhs, rhs, ((1,), (0,)))
            row_weight = [
                jnp.where(rows == r, a0, jnp.where(rows == r - 1, a1, 0.0))
                for r in range(begin, stop)
            ]
            profile = jnp.zeros((PAD, width), jnp.float32)
            for k in range(stop - begin):
                profile = profile + row_weight[k] * taken[k * PAD : (k + 1) * PAD]
            weighted = jnp.where(keep, obs[t, band] * profile, 0.0)
            spread = jnp.concatenate(
                [row_weight[r - begin] * weighted for r in range(lo, hi)], 0
            )
            added = dot3(split(spread), rhs, ((1,), (1,)))
            adj[lo:hi] += added.reshape(hi - lo, PAD, width)
            return 0

        lax.fori_loop(0, 3, tile_of, 0)

    diffuse_all(adj, other, coef, 6, BAND - 6)

    eoft = eoft_ref[...]
    rr = dim = rim = imim = jnp.zeros((levels, LANES), jnp.float32)
    for r in range(ROWS):
        back = jnp.dot(
            eoft, other[ROWS + r, :levels, :LANES], precision=HIGHEST, preferred_element_type=jnp.float32
        )
        d, res = dir_ref[:, r, :], res_ref[:, r, :]
        image = d + back
        img_ref[:, r, :] = image
        rr, dim, rim, imim = rr + res * res, dim + d * image, rim + res * image, imim + image * image
    lane = lax.broadcasted_iota(jnp.int32, part_ref.shape, 1)
    out = jnp.zeros(part_ref.shape, jnp.float32)
    for k, value in enumerate((rr, dim, rim, imim)):
        out = jnp.where(lane == k, jnp.sum(value), out)
    part_ref[...] = out


def finish(part_ref, img_ref, res_ref, dir_ref, new_res_ref, new_dir_ref, step_ref):
    total = jnp.sum(part_ref[...], axis=0, keepdims=True)
    lane = lax.broadcasted_iota(jnp.int32, total.shape, 1)
    rr, dim, rim, imim = (
        jnp.sum(jnp.where(lane == k, total, 0.0), axis=1, keepdims=True) for k in range(4)
    )
    step = rr / dim
    new_norm = rr + step * (step * imim - 2.0 * rim)
    beta = new_norm / rr
    step_ref[...] = step
    new_res = res_ref[...] - step[None] * img_ref[...]
    new_res_ref[...] = new_res
    new_dir_ref[...] = new_res + beta[None] * dir_ref[...]


def lat_pairs(lon_count, lat_count):
    index = lambda lon, lat: lon * lat_count + lat
    first, second = [], []
    for lon in range(lon_count):
        for lat in range(lat_count):
            first.append((index(lon, lat), index(lon, lat ^ 1)))
            other = lat + 1 if lat % 2 else lat - 1
            if other == lat_count:
                second.append((index(lon, lat), index(lon_count - 1 - lon, lat)))
            elif other >= 0:
                second.append((index(lon, lat), index(lon, other)))
    return first, second


def lon_pairs(lon_count):
    first = [(lon, lon ^ 1) for lon in range(lon_count)]
    second = [(lon, (lon + 1 if lon % 2 else lon - 1) % lon_count) for lon in range(lon_count)]
    return first, second


def per_device(
    direction, residual, eof_basis, kappa_east, kappa_north, wet_mask, obs_base, obs_frac, obs_rinv
):
    levels = direction.shape[0]
    shape = functools.partial(jax.ShapeDtypeStruct, dtype=jnp.float32)
    lon_count, lat_count = lax.axis_size("lon"), lax.axis_size("lat")
    lon, lat = lax.axis_index("lon"), lax.axis_index("lat")
    flags = jnp.stack([1 - lat % 2, 1 - lon % 2, (lat == lat_count - 1).astype(jnp.int32)])
    flags = flags.astype(jnp.int32)
    own = pl.pallas_call(
        pack_tile, out_shape=shape((ROWS + 2, PAD, LANES)), in_specs=[VMEM] * 8, out_specs=VMEM
    )(
        eof_basis,
        direction,
        kappa_east,
        kappa_north,
        wet_mask,
        obs_base.reshape(1, -1),
        obs_frac.reshape(2, -1),
        obs_rinv.reshape(levels, -1),
    )
    first, second = lat_pairs(lon_count, lat_count)
    lat_b = lax.ppermute(own, ("lon", "lat"), second)
    lat_a = lax.ppermute(own, ("lon", "lat"), first)
    north_south, to_a, to_b = pl.pallas_call(
        pack_columns,
        out_shape=(shape((2, ROWS + 2, PAD, LANES)), shape((8, PAD, LANES)), shape((8, PAD, LANES))),
        in_specs=[SMEM] + [VMEM] * 3,
        out_specs=(VMEM,) * 3,
    )(flags, own, lat_a, lat_b)
    first, second = lon_pairs(lon_count)
    lon_b = lax.ppermute(to_b, "lon", second)
    lon_a = lax.ppermute(to_a, "lon", first)
    image, part = pl.pallas_call(
        local_image,
        out_shape=(shape(direction.shape), shape((lon_count, LANES))),
        in_specs=[SMEM] + [VMEM] * 7,
        out_specs=(VMEM,) * 2,
        scratch_shapes=[
            pltpu.VMEM((BAND, PAD, 2 * LANES), jnp.float32),
            pltpu.VMEM((BAND, PAD, 2 * LANES), jnp.float32),
            pltpu.VMEM((BAND, PAD, 2 * LANES), jnp.float32),
            pltpu.VMEM((5, BAND, 2 * LANES), jnp.float32),
            pltpu.VMEM((3, 3, PAD, 2 * LANES), jnp.float32),
        ],
    )(flags, own, north_south, lon_a, lon_b, direction, residual, eof_basis.T)
    part = lax.all_to_all(part, "lon", 0, 0, tiled=True)
    part = jnp.broadcast_to(jnp.sum(part, axis=0, keepdims=True), (lat_count, LANES))
    part = lax.all_to_all(part, "lat", 0, 0, tiled=True)
    new_residual, new_direction, step_length = pl.pallas_call(
        finish,
        out_shape=(shape(direction.shape), shape(direction.shape), shape((1, 1))),
        in_specs=[VMEM] * 4,
        out_specs=(VMEM,) * 3,
    )(part, image, residual, direction)
    return new_residual, new_direction, step_length.reshape(())


def solution(mesh):
    return jax.shard_map(
        per_device,
        mesh=mesh,
        in_specs=(
            P(None, "lat", "lon"),
            P(None, "lat", "lon"),
            P(),
            P("lat", "lon"),
            P("lat", "lon"),
            P("lat", "lon"),
            P("lat", "lon", None),
            P(None, "lat", "lon", None),
            P(None, "lat", "lon", None),
        ),
        out_specs=(P(None, "lat", "lon"), P(None, "lat", "lon"), P()),
        check_vma=False,
    )
```

```python
import functools

import jax
import jax.numpy as jnp
from jax import lax
from jax.experimental import pallas as pl
from jax.experimental.pallas import tpu as pltpu
from jax.sharding import PartitionSpec as P


HIGHEST = lax.Precision.HIGHEST
LANES = 128
ROWS = 8
PAD = 80
BAND = 3 * ROWS
HALO = 7
SLOTS = 12
SOUTH, OWN, NORTH = 0, 1, 2

SMEM = pl.BlockSpec(memory_space=pltpu.SMEM)
VMEM = pl.BlockSpec(memory_space=pltpu.VMEM)


def grant(mebibytes):
    return pltpu.CompilerParams(vmem_limit_bytes=mebibytes << 20)


def near(x):
    return pltpu.with_memory_space_constraint(x, pltpu.VMEM)


def split(x):
    high = x.astype(jnp.bfloat16)
    return high, (x - high.astype(jnp.float32)).astype(jnp.bfloat16)


def dot3(left, right, dims):
    (lh, ll), (rh, rl) = left, right
    mul = functools.partial(
        lax.dot_general, dimension_numbers=(dims, ((), ())), preferred_element_type=jnp.float32
    )
    return mul(lh, rh) + (mul(lh, rl) + mul(ll, rh))


def pack_tile(eof_ref, dir_ref, ke_ref, kn_ref, wet_ref, base_ref, frac_ref, rinv_ref, out_ref):
    levels = dir_ref.shape[0]
    zeros = jnp.zeros((PAD - levels - 3, LANES), jnp.float32)
    eof = eof_ref[...]
    for row in range(ROWS):
        out_ref[row, :levels, :] = jnp.dot(
            eof, dir_ref[:, row, :], precision=HIGHEST, preferred_element_type=jnp.float32
        )
        out_ref[row, levels : levels + 1, :] = ke_ref[row : row + 1, :]
        out_ref[row, levels + 1 : levels + 2, :] = kn_ref[row : row + 1, :]
        out_ref[row, levels + 2 : levels + 3, :] = wet_ref[row : row + 1, :].astype(jnp.float32)
        out_ref[row, levels + 3 :, :] = zeros
    for half in range(2):
        cut = slice(half * LANES, (half + 1) * LANES)
        for level in range(levels):
            out_ref[ROWS + half, level : level + 1, :] = rinv_ref[level, :, cut]
        out_ref[ROWS + half, levels : levels + 1, :] = base_ref[:, cut].astype(jnp.float32)
        out_ref[ROWS + half, levels + 1 : levels + 2, :] = frac_ref[0, :, cut]
        out_ref[ROWS + half, levels + 2 : levels + 3, :] = frac_ref[1, :, cut]
        out_ref[ROWS + half, levels + 3 :, :] = zeros


def pack_columns(flags, own_ref, ra_ref, rb_ref, ns_ref, pa_ref, pb_ref):
    lat_even, lon_even, is_top = flags[0] == 1, flags[1] == 1, flags[2] == 1

    @pl.when(lat_even)
    def _():
        ns_ref[0] = ra_ref[...]
        ns_ref[1] = rb_ref[...]

    @pl.when(jnp.logical_not(lat_even))
    def _():
        ns_ref[0] = rb_ref[...]
        ns_ref[1] = ra_ref[...]

    @pl.when(is_top)
    def _():
        first = lax.broadcasted_iota(jnp.int32, (LANES, LANES), 0)
        second = lax.broadcasted_iota(jnp.int32, (LANES, LANES), 1)
        flip = jnp.where(first + second == LANES - 1, 1.0, 0.0).astype(jnp.float32)
        for row in range(ROWS):
            ns_ref[0, row] = jnp.dot(
                rb_ref[ROWS - 1 - row], flip, precision=HIGHEST, preferred_element_type=jnp.float32
            )

    lane = lax.broadcasted_iota(jnp.int32, (8, LANES), 1)

    def one(step, _):
        cut = pl.ds(pl.multiple_of(step * 8, 8), 8)
        for group in range(2):
            west = jnp.zeros((8, LANES), jnp.float32)
            east = jnp.zeros((8, LANES), jnp.float32)
            for slot in range(SLOTS):
                index = group * SLOTS + slot
                if index < ROWS:
                    tile = ns_ref[1, index, cut, :]
                elif index < 2 * ROWS:
                    tile = own_ref[index - ROWS, cut, :]
                else:
                    tile = ns_ref[0, index - 2 * ROWS, cut, :]
                start = HALO * slot
                here = (lane >= start) & (lane < start + HALO)
                west = jnp.where(here, pltpu.roll(tile, start, 1) if start else tile, west)
                east = jnp.where(here, pltpu.roll(tile, (start + HALO) % LANES, 1), east)
            pa_ref[group, cut, :] = jnp.where(lon_even, east, west)
            pb_ref[group, cut, :] = jnp.where(lon_even, west, east)
        return 0

    lax.fori_loop(0, PAD // 8, one, 0)
    for half in range(2):
        for ref in (pa_ref, pb_ref):
            ref[2 + 2 * SOUTH + half] = ns_ref[1, ROWS + half]
            ref[2 + 2 * OWN + half] = own_ref[ROWS + half]
            ref[2 + 2 * NORTH + half] = ns_ref[0, ROWS + half]


def diffuse_row(src, dst, coef, index, cut):
    centre = src[index, cut, :]
    width = centre.shape[1]
    wide = lambda k: jnp.broadcast_to(coef[k, pl.ds(index, 1), :], centre.shape)
    out = centre * wide(0)
    out = out + wide(1) * pltpu.roll(centre, width - 1, 1)
    out = out + wide(2) * pltpu.roll(centre, 1, 1)
    out = out + wide(3) * src[index + 1, cut, :]
    out = out + wide(4) * src[index - 1, cut, :]
    dst[index, cut, :] = out


def diffuse_all(one, two, coef, low, high):
    def body(step, _):
        cut = pl.ds(pl.multiple_of(step * 8, 8), 8)
        for src, dst, trim in ((one, two, 0), (two, one, 1), (one, two, 2)):
            for index in range(low + trim, high - trim):
                diffuse_row(src, dst, coef, index, cut)
        return 0

    lax.fori_loop(0, PAD // 8, body, 0)


def local_image(
    flags,
    own_ref,
    ns_ref,
    qa_ref,
    qb_ref,
    dir_ref,
    res_ref,
    eoft_ref,
    img_ref,
    part_ref,
    field,
    other,
    adj,
    coef,
    obs,
):
    lon_even, is_top = flags[1] == 1, flags[2] == 1
    levels = dir_ref.shape[0]
    width = 2 * LANES
    lane = lax.broadcasted_iota(jnp.int32, (8, LANES), 1)

    def unpack(step, _):
        cut = pl.ds(pl.multiple_of(step * 8, 8), 8)
        for group in range(2):
            first, second = qa_ref[group, cut, :], qb_ref[group, cut, :]
            east = jnp.where(lon_even, first, second)
            west = jnp.where(lon_even, second, first)
            for slot in range(SLOTS):
                index = group * SLOTS + slot
                if index < ROWS:
                    tile = ns_ref[1, index, cut, :]
                elif index < 2 * ROWS:
                    tile = own_ref[index - ROWS, cut, :]
                else:
                    tile = ns_ref[0, index - 2 * ROWS, cut, :]
                start = HALO * slot
                from_east = pltpu.roll(east, (LANES - start) % LANES, 1) if start else east
                from_west = pltpu.roll(west, (LANES - HALO - start) % LANES, 1)
                halo = jnp.where(
                    lane < HALO, from_east, jnp.where(lane >= LANES - HALO, from_west, 0.0)
                )
                field[index, cut, :LANES] = tile
                field[index, cut, LANES:] = halo
        return 0

    lax.fori_loop(0, PAD // 8, unpack, 0)

    ke, kn, wet = field[:, levels, :], field[:, levels + 1, :], field[:, levels + 2, :]
    row = lax.broadcasted_iota(jnp.int32, (BAND, width), 0)
    up = lambda x: jnp.concatenate([x[1:], x[:1]], 0)
    down = lambda x: jnp.concatenate([x[-1:], x[:-1]], 0)
    right = lambda x: pltpu.roll(x, width - 1, 1)
    left = lambda x: pltpu.roll(x, 1, 1)
    seam = 2 * ROWS - 1
    top = jnp.where(is_top, 1, 0)
    ke = jnp.where((row > seam) & (top == 1), right(ke), ke)
    kn_up = up(kn)
    kn = jnp.where(
        top == 1, jnp.where(row > seam, kn_up, jnp.where(row == seam, 0.5 * (kn + kn_up), kn)), kn
    )
    east_face = ke * wet * right(wet)
    north_face = kn * wet * up(wet)
    west_face, south_face = left(east_face), down(north_face)
    coef[0] = 1.0 - east_face - west_face - north_face - south_face
    coef[1] = east_face
    coef[2] = west_face
    coef[3] = north_face
    coef[4] = south_face

    diffuse_all(field, other, coef, 2, BAND - 2)
    physical = other

    keep = lax.broadcasted_iota(jnp.int32, (PAD, LANES), 0) < levels
    for band in range(3):
        for half in range(2):
            cut = slice(half * LANES, (half + 1) * LANES)
            slot = 2 + 2 * band + half
            first, second = qa_ref[slot], qb_ref[slot]
            mid = (ns_ref[1, ROWS + half], own_ref[ROWS + half], ns_ref[0, ROWS + half])[band]
            obs[0, band, :, cut] = jnp.where(lon_even, second, first)
            obs[1, band, :, cut] = mid
            obs[2, band, :, cut] = jnp.where(lon_even, first, second)
    adj[...] = jnp.zeros(adj.shape, jnp.float32)
    cells = lax.broadcasted_iota(jnp.int32, (width, width), 0)
    keep = lax.broadcasted_iota(jnp.int32, (PAD, width), 0) < levels
    spans = ((4, 9, 5), (8, 17, 8), (16, 20, 16))
    ends = (9, 17, 19)
    for band in range(3):
        begin, stop, adj_begin = spans[band]
        adj_stop = ends[band]
        lhs = split(physical[begin:stop].reshape((stop - begin) * PAD, width))

        def tile_of(t, _, band=band, lhs=lhs, begin=begin, stop=stop, lo=adj_begin, hi=adj_stop):
            base = obs[t, band, levels : levels + 1, :].astype(jnp.int32)
            p = obs[t, band, levels + 1 : levels + 2, :]
            q = obs[t, band, levels + 2 : levels + 3, :]
            j, i = base >> 7, base & (LANES - 1)
            rows, cols = j + ROWS * band, i
            a0, a1, b0, b1 = 1.0 - p, p, 1.0 - q, q
            if band == NORTH:
                turned = top == 1
                rows = jnp.where(turned, 22 - j, rows)
                cols = jnp.where(turned, 126 - i, cols)
                a0, a1 = jnp.where(turned, a1, a0), jnp.where(turned, a0, a1)
                b0, b1 = jnp.where(turned, b1, b0), jnp.where(turned, b0, b1)
            near = jnp.where(t == 1, 1, jnp.where(t == 0, jnp.where(cols >= 64, 1, 0), jnp.where(cols < 64, 1, 0)))
            b0, b1 = jnp.where(near == 1, b0, 0.0), jnp.where(near == 1, b1, 0.0)
            lane0 = (cols + jnp.where(t == 1, 0, LANES)) & (width - 1)
            lane1 = (lane0 + 1) & (width - 1)
            weight = jnp.where(cells == lane0, b0, jnp.where(cells == lane1, b1, 0.0))
            rhs = split(weight)
            taken = dot3(lhs, rhs, ((1,), (0,)))
            row_weight = [
                jnp.where(rows == r, a0, jnp.where(rows == r - 1, a1, 0.0))
                for r in range(begin, stop)
            ]
            profile = jnp.zeros((PAD, width), jnp.float32)
            for k in range(stop - begin):
                profile = profile + row_weight[k] * taken[k * PAD : (k + 1) * PAD]
            weighted = jnp.where(keep, obs[t, band] * profile, 0.0)
            spread = jnp.concatenate(
                [row_weight[r - begin] * weighted for r in range(lo, hi)], 0
            )
            added = dot3(split(spread), rhs, ((1,), (1,)))
            adj[lo:hi] += added.reshape(hi - lo, PAD, width)
            return 0

        lax.fori_loop(0, 3, tile_of, 0)

    diffuse_all(adj, other, coef, 6, BAND - 6)

    eoft = eoft_ref[...]
    rr = dim = rim = imim = jnp.zeros((levels, LANES), jnp.float32)
    for r in range(ROWS):
        back = jnp.dot(
            eoft, other[ROWS + r, :levels, :LANES], precision=HIGHEST, preferred_element_type=jnp.float32
        )
        d, res = dir_ref[:, r, :], res_ref[:, r, :]
        image = d + back
        img_ref[:, r, :] = image
        rr, dim, rim, imim = rr + res * res, dim + d * image, rim + res * image, imim + image * image
    lane = lax.broadcasted_iota(jnp.int32, part_ref.shape, 1)
    out = jnp.zeros(part_ref.shape, jnp.float32)
    for k, value in enumerate((rr, dim, rim, imim)):
        out = jnp.where(lane == k, jnp.sum(value), out)
    part_ref[...] = out


def finish(part_ref, img_ref, res_ref, dir_ref, new_res_ref, new_dir_ref, step_ref):
    total = jnp.sum(part_ref[...], axis=0, keepdims=True)
    lane = lax.broadcasted_iota(jnp.int32, total.shape, 1)
    rr, dim, rim, imim = (
        jnp.sum(jnp.where(lane == k, total, 0.0), axis=1, keepdims=True) for k in range(4)
    )
    step = rr / dim
    new_norm = rr + step * (step * imim - 2.0 * rim)
    beta = new_norm / rr
    step_ref[...] = step
    new_res = res_ref[...] - step[None] * img_ref[...]
    new_res_ref[...] = new_res
    new_dir_ref[...] = new_res + beta[None] * dir_ref[...]


def lat_pairs(lon_count, lat_count):
    index = lambda lon, lat: lon * lat_count + lat
    first, second = [], []
    for lon in range(lon_count):
        for lat in range(lat_count):
            first.append((index(lon, lat), index(lon, lat ^ 1)))
            other = lat + 1 if lat % 2 else lat - 1
            if other == lat_count:
                second.append((index(lon, lat), index(lon_count - 1 - lon, lat)))
            elif other >= 0:
                second.append((index(lon, lat), index(lon, other)))
    return first, second


def lon_pairs(lon_count):
    first = [(lon, lon ^ 1) for lon in range(lon_count)]
    second = [(lon, (lon + 1 if lon % 2 else lon - 1) % lon_count) for lon in range(lon_count)]
    return first, second


def per_device(
    direction, residual, eof_basis, kappa_east, kappa_north, wet_mask, obs_base, obs_frac, obs_rinv
):
    levels = direction.shape[0]
    shape = functools.partial(jax.ShapeDtypeStruct, dtype=jnp.float32)
    local = functools.partial(pltpu.VMEM, dtype=jnp.float32)
    lon_count, lat_count = lax.axis_size("lon"), lax.axis_size("lat")
    lon, lat = lax.axis_index("lon"), lax.axis_index("lat")
    flags = jnp.stack([1 - lat % 2, 1 - lon % 2, (lat == lat_count - 1).astype(jnp.int32)])
    flags = flags.astype(jnp.int32)
    direction, residual = near(direction), near(residual)
    own = pl.pallas_call(
        pack_tile, out_shape=local((ROWS + 2, PAD, LANES)), in_specs=[VMEM] * 8, out_specs=VMEM,
        compiler_params=grant(8),
    )(
        eof_basis,
        direction,
        kappa_east,
        kappa_north,
        wet_mask,
        obs_base.reshape(1, -1),
        obs_frac.reshape(2, 1, -1),
        obs_rinv.reshape(levels, 1, -1),
    )
    first, second = lat_pairs(lon_count, lat_count)
    lat_b = lax.ppermute(own, ("lon", "lat"), second)
    lat_a = lax.ppermute(own, ("lon", "lat"), first)
    own, lat_a, lat_b = near(own), near(lat_a), near(lat_b)
    north_south, to_a, to_b = pl.pallas_call(
        pack_columns,
        out_shape=(local((2, ROWS + 2, PAD, LANES)), local((8, PAD, LANES)), local((8, PAD, LANES))),
        in_specs=[SMEM] + [VMEM] * 3,
        out_specs=(VMEM,) * 3,
        compiler_params=grant(8),
    )(flags, own, lat_a, lat_b)
    first, second = lon_pairs(lon_count)
    lon_b = lax.ppermute(to_b, "lon", second)
    lon_a = lax.ppermute(to_a, "lon", first)
    image, part = pl.pallas_call(
        local_image,
        out_shape=(local(direction.shape), local((lon_count, LANES))),
        in_specs=[SMEM] + [VMEM] * 7,
        out_specs=(VMEM,) * 2,
        compiler_params=grant(28),
        scratch_shapes=[
            pltpu.VMEM((BAND, PAD, 2 * LANES), jnp.float32),
            pltpu.VMEM((BAND, PAD, 2 * LANES), jnp.float32),
            pltpu.VMEM((BAND, PAD, 2 * LANES), jnp.float32),
            pltpu.VMEM((5, BAND, 2 * LANES), jnp.float32),
            pltpu.VMEM((3, 3, PAD, 2 * LANES), jnp.float32),
        ],
    )(flags, own, near(north_south), near(lon_a), near(lon_b), direction, residual, near(eof_basis.T))
    part = lax.all_to_all(part, "lon", 0, 0, tiled=True)
    part = jnp.broadcast_to(jnp.sum(part, axis=0, keepdims=True), (lat_count, LANES))
    part = lax.all_to_all(part, "lat", 0, 0, tiled=True)
    new_residual, new_direction, step_length = pl.pallas_call(
        finish,
        out_shape=(shape(direction.shape), shape(direction.shape), shape((1, 1))),
        in_specs=[VMEM] * 4,
        out_specs=(VMEM,) * 3,
        compiler_params=grant(8),
    )(near(part), near(image), residual, direction)
    return new_residual, new_direction, step_length.reshape(())


def solution(mesh):
    return jax.shard_map(
        per_device,
        mesh=mesh,
        in_specs=(
            P(None, "lat", "lon"),
            P(None, "lat", "lon"),
            P(),
            P("lat", "lon"),
            P("lat", "lon"),
            P("lat", "lon"),
            P("lat", "lon", None),
            P(None, "lat", "lon", None),
            P(None, "lat", "lon", None),
        ),
        out_specs=(P(None, "lat", "lon"), P(None, "lat", "lon"), P()),
        check_vma=False,
    )
```

```python
import functools

import jax
import jax.numpy as jnp
from jax import lax
from jax.experimental import pallas as pl
from jax.experimental.pallas import tpu as pltpu
from jax.sharding import PartitionSpec as P


HIGHEST = lax.Precision.HIGHEST
LANES = 128
ROWS = 8
PAD = 80
BAND = 3 * ROWS
HALO = 7
SLOTS = 12
SOUTH, OWN, NORTH = 0, 1, 2

SMEM = pl.BlockSpec(memory_space=pltpu.SMEM)
VMEM = pl.BlockSpec(memory_space=pltpu.VMEM)


def grant(mebibytes):
    return pltpu.CompilerParams(vmem_limit_bytes=mebibytes << 20)


def near(x):
    return pltpu.with_memory_space_constraint(x, pltpu.VMEM)


def split(x):
    high = x.astype(jnp.bfloat16)
    return high, (x - high.astype(jnp.float32)).astype(jnp.bfloat16)


def dot3(left, right, dims):
    (lh, ll), (rh, rl) = left, right
    mul = functools.partial(
        lax.dot_general, dimension_numbers=(dims, ((), ())), preferred_element_type=jnp.float32
    )
    return mul(lh, rh) + (mul(lh, rl) + mul(ll, rh))


def pack_tile(*refs):
    count = (len(refs) - 2) // 2
    sources, out_ref, held, sems = refs[:count], refs[count], refs[count + 1 : -1], refs[-1]
    copies = [
        pltpu.make_async_copy(source, target, sems.at[k])
        for k, (source, target) in enumerate(zip(sources, held))
    ]
    for copy in copies:
        copy.start()
    for copy in copies:
        copy.wait()
    dir_ref, eof_ref, ke_ref, kn_ref, wet_ref, base_ref, frac_ref, rinv_ref = held
    levels = dir_ref.shape[0]
    zeros = jnp.zeros((PAD - levels - 3, LANES), jnp.float32)
    eof = eof_ref[...]
    for row in range(ROWS):
        out_ref[row, :levels, :] = jnp.dot(
            eof, dir_ref[:, row, :], precision=HIGHEST, preferred_element_type=jnp.float32
        )
        out_ref[row, levels : levels + 1, :] = ke_ref[row : row + 1, :]
        out_ref[row, levels + 1 : levels + 2, :] = kn_ref[row : row + 1, :]
        out_ref[row, levels + 2 : levels + 3, :] = wet_ref[row : row + 1, :].astype(jnp.float32)
        out_ref[row, levels + 3 :, :] = zeros
    for half in range(2):
        cut = slice(half * LANES, (half + 1) * LANES)
        for level in range(levels):
            out_ref[ROWS + half, level : level + 1, :] = rinv_ref[level, :, cut]
        out_ref[ROWS + half, levels : levels + 1, :] = base_ref[:, cut].astype(jnp.float32)
        out_ref[ROWS + half, levels + 1 : levels + 2, :] = frac_ref[0, :, cut]
        out_ref[ROWS + half, levels + 2 : levels + 3, :] = frac_ref[1, :, cut]
        out_ref[ROWS + half, levels + 3 :, :] = zeros


def pack_columns(flags, own_ref, ra_ref, rb_ref, ns_ref, pa_ref, pb_ref):
    lat_even, lon_even, is_top = flags[0] == 1, flags[1] == 1, flags[2] == 1

    @pl.when(lat_even)
    def _():
        ns_ref[0] = ra_ref[...]
        ns_ref[1] = rb_ref[...]

    @pl.when(jnp.logical_not(lat_even))
    def _():
        ns_ref[0] = rb_ref[...]
        ns_ref[1] = ra_ref[...]

    @pl.when(is_top)
    def _():
        first = lax.broadcasted_iota(jnp.int32, (LANES, LANES), 0)
        second = lax.broadcasted_iota(jnp.int32, (LANES, LANES), 1)
        flip = jnp.where(first + second == LANES - 1, 1.0, 0.0).astype(jnp.float32)
        for row in range(ROWS):
            ns_ref[0, row] = jnp.dot(
                rb_ref[ROWS - 1 - row], flip, precision=HIGHEST, preferred_element_type=jnp.float32
            )

    lane = lax.broadcasted_iota(jnp.int32, (8, LANES), 1)

    def one(step, _):
        cut = pl.ds(pl.multiple_of(step * 8, 8), 8)
        for group in range(2):
            west = jnp.zeros((8, LANES), jnp.float32)
            east = jnp.zeros((8, LANES), jnp.float32)
            for slot in range(SLOTS):
                index = group * SLOTS + slot
                if index < ROWS:
                    tile = ns_ref[1, index, cut, :]
                elif index < 2 * ROWS:
                    tile = own_ref[index - ROWS, cut, :]
                else:
                    tile = ns_ref[0, index - 2 * ROWS, cut, :]
                start = HALO * slot
                here = (lane >= start) & (lane < start + HALO)
                west = jnp.where(here, pltpu.roll(tile, start, 1) if start else tile, west)
                east = jnp.where(here, pltpu.roll(tile, (start + HALO) % LANES, 1), east)
            pa_ref[group, cut, :] = jnp.where(lon_even, east, west)
            pb_ref[group, cut, :] = jnp.where(lon_even, west, east)
        return 0

    lax.fori_loop(0, PAD // 8, one, 0)
    for half in range(2):
        for ref in (pa_ref, pb_ref):
            ref[2 + 2 * SOUTH + half] = ns_ref[1, ROWS + half]
            ref[2 + 2 * OWN + half] = own_ref[ROWS + half]
            ref[2 + 2 * NORTH + half] = ns_ref[0, ROWS + half]


def diffuse_row(src, dst, coef, index, cut):
    centre = src[index, cut, :]
    width = centre.shape[1]
    wide = lambda k: jnp.broadcast_to(coef[k, pl.ds(index, 1), :], centre.shape)
    out = centre * wide(0)
    out = out + wide(1) * pltpu.roll(centre, width - 1, 1)
    out = out + wide(2) * pltpu.roll(centre, 1, 1)
    out = out + wide(3) * src[index + 1, cut, :]
    out = out + wide(4) * src[index - 1, cut, :]
    dst[index, cut, :] = out


def diffuse_all(one, two, coef, low, high):
    def body(step, _):
        cut = pl.ds(pl.multiple_of(step * 16, 16), 16)
        for src, dst, trim in ((one, two, 0), (two, one, 1), (one, two, 2)):
            for index in range(low + trim, high - trim):
                diffuse_row(src, dst, coef, index, cut)
        return 0

    lax.fori_loop(0, PAD // 16, body, 0)


def local_image(
    flags,
    own_ref,
    ns_ref,
    qa_ref,
    qb_ref,
    dir_ref,
    res_ref,
    eoft_ref,
    img_ref,
    part_ref,
    field,
    other,
    adj,
    coef,
    obs,
):
    lon_even, is_top = flags[1] == 1, flags[2] == 1
    levels = dir_ref.shape[0]
    width = 2 * LANES
    lane = lax.broadcasted_iota(jnp.int32, (8, LANES), 1)

    def unpack(step, _):
        cut = pl.ds(pl.multiple_of(step * 8, 8), 8)
        for group in range(2):
            first, second = qa_ref[group, cut, :], qb_ref[group, cut, :]
            east = jnp.where(lon_even, first, second)
            west = jnp.where(lon_even, second, first)
            for slot in range(SLOTS):
                index = group * SLOTS + slot
                if index < ROWS:
                    tile = ns_ref[1, index, cut, :]
                elif index < 2 * ROWS:
                    tile = own_ref[index - ROWS, cut, :]
                else:
                    tile = ns_ref[0, index - 2 * ROWS, cut, :]
                start = HALO * slot
                from_east = pltpu.roll(east, (LANES - start) % LANES, 1) if start else east
                from_west = pltpu.roll(west, (LANES - HALO - start) % LANES, 1)
                halo = jnp.where(
                    lane < HALO, from_east, jnp.where(lane >= LANES - HALO, from_west, 0.0)
                )
                field[index, cut, :LANES] = tile
                field[index, cut, LANES:] = halo
        return 0

    lax.fori_loop(0, PAD // 8, unpack, 0)

    ke, kn, wet = field[:, levels, :], field[:, levels + 1, :], field[:, levels + 2, :]
    row = lax.broadcasted_iota(jnp.int32, (BAND, width), 0)
    up = lambda x: jnp.concatenate([x[1:], x[:1]], 0)
    down = lambda x: jnp.concatenate([x[-1:], x[:-1]], 0)
    right = lambda x: pltpu.roll(x, width - 1, 1)
    left = lambda x: pltpu.roll(x, 1, 1)
    seam = 2 * ROWS - 1
    top = jnp.where(is_top, 1, 0)
    ke = jnp.where((row > seam) & (top == 1), right(ke), ke)
    kn_up = up(kn)
    kn = jnp.where(
        top == 1, jnp.where(row > seam, kn_up, jnp.where(row == seam, 0.5 * (kn + kn_up), kn)), kn
    )
    east_face = ke * wet * right(wet)
    north_face = kn * wet * up(wet)
    west_face, south_face = left(east_face), down(north_face)
    coef[0] = 1.0 - east_face - west_face - north_face - south_face
    coef[1] = east_face
    coef[2] = west_face
    coef[3] = north_face
    coef[4] = south_face

    diffuse_all(field, other, coef, 2, BAND - 2)
    physical = other

    keep = lax.broadcasted_iota(jnp.int32, (PAD, LANES), 0) < levels
    for band in range(3):
        for half in range(2):
            cut = slice(half * LANES, (half + 1) * LANES)
            slot = 2 + 2 * band + half
            first, second = qa_ref[slot], qb_ref[slot]
            mid = (ns_ref[1, ROWS + half], own_ref[ROWS + half], ns_ref[0, ROWS + half])[band]
            obs[0, band, :, cut] = jnp.where(lon_even, second, first)
            obs[1, band, :, cut] = mid
            obs[2, band, :, cut] = jnp.where(lon_even, first, second)
    adj[...] = jnp.zeros(adj.shape, jnp.float32)
    cells = lax.broadcasted_iota(jnp.int32, (width, width), 0)
    keep = lax.broadcasted_iota(jnp.int32, (PAD, width), 0) < levels
    spans = ((4, 9, 5), (8, 17, 8), (16, 20, 16))
    ends = (9, 17, 19)
    for band in range(3):
        begin, stop, adj_begin = spans[band]
        adj_stop = ends[band]
        lhs = split(physical[begin:stop].reshape((stop - begin) * PAD, width))

        def tile_of(t, _, band=band, lhs=lhs, begin=begin, stop=stop, lo=adj_begin, hi=adj_stop):
            base = obs[t, band, levels : levels + 1, :].astype(jnp.int32)
            p = obs[t, band, levels + 1 : levels + 2, :]
            q = obs[t, band, levels + 2 : levels + 3, :]
            j, i = base >> 7, base & (LANES - 1)
            rows, cols = j + ROWS * band, i
            a0, a1, b0, b1 = 1.0 - p, p, 1.0 - q, q
            if band == NORTH:
                turned = top == 1
                rows = jnp.where(turned, 22 - j, rows)
                cols = jnp.where(turned, 126 - i, cols)
                a0, a1 = jnp.where(turned, a1, a0), jnp.where(turned, a0, a1)
                b0, b1 = jnp.where(turned, b1, b0), jnp.where(turned, b0, b1)
            near = jnp.where(t == 1, 1, jnp.where(t == 0, jnp.where(cols >= 64, 1, 0), jnp.where(cols < 64, 1, 0)))
            b0, b1 = jnp.where(near == 1, b0, 0.0), jnp.where(near == 1, b1, 0.0)
            lane0 = (cols + jnp.where(t == 1, 0, LANES)) & (width - 1)
            lane1 = (lane0 + 1) & (width - 1)
            weight = jnp.where(cells == lane0, b0, jnp.where(cells == lane1, b1, 0.0))
            rhs = split(weight)
            taken = dot3(lhs, rhs, ((1,), (0,)))
            row_weight = [
                jnp.where(rows == r, a0, jnp.where(rows == r - 1, a1, 0.0))
                for r in range(begin, stop)
            ]
            profile = jnp.zeros((PAD, width), jnp.float32)
            for k in range(stop - begin):
                profile = profile + row_weight[k] * taken[k * PAD : (k + 1) * PAD]
            weighted = jnp.where(keep, obs[t, band] * profile, 0.0)
            spread = jnp.concatenate(
                [row_weight[r - begin] * weighted for r in range(lo, hi)], 0
            )
            added = dot3(split(spread), rhs, ((1,), (1,)))
            adj[lo:hi] += added.reshape(hi - lo, PAD, width)
            return 0

        lax.fori_loop(0, 3, tile_of, 0)

    diffuse_all(adj, other, coef, 6, BAND - 6)

    eoft = eoft_ref[...]
    rr = dim = rim = imim = jnp.zeros((levels, LANES), jnp.float32)
    for r in range(ROWS):
        back = jnp.dot(
            eoft, other[ROWS + r, :levels, :LANES], precision=HIGHEST, preferred_element_type=jnp.float32
        )
        d, res = dir_ref[:, r, :], res_ref[:, r, :]
        image = d + back
        img_ref[:, r, :] = image
        rr, dim, rim, imim = rr + res * res, dim + d * image, rim + res * image, imim + image * image
    lane = lax.broadcasted_iota(jnp.int32, part_ref.shape, 1)
    out = jnp.zeros(part_ref.shape, jnp.float32)
    for k, value in enumerate((rr, dim, rim, imim)):
        out = jnp.where(lane == k, jnp.sum(value), out)
    part_ref[...] = out


def finish(part_ref, img_ref, res_ref, dir_ref, new_res_ref, new_dir_ref, step_ref):
    total = jnp.sum(part_ref[...], axis=0, keepdims=True)
    lane = lax.broadcasted_iota(jnp.int32, total.shape, 1)
    rr, dim, rim, imim = (
        jnp.sum(jnp.where(lane == k, total, 0.0), axis=1, keepdims=True) for k in range(4)
    )
    step = rr / dim
    new_norm = rr + step * (step * imim - 2.0 * rim)
    beta = new_norm / rr
    step_ref[...] = step
    new_res = res_ref[...] - step[None] * img_ref[...]
    new_res_ref[...] = new_res
    new_dir_ref[...] = new_res + beta[None] * dir_ref[...]


def lat_pairs(lon_count, lat_count):
    index = lambda lon, lat: lon * lat_count + lat
    first, second = [], []
    for lon in range(lon_count):
        for lat in range(lat_count):
            first.append((index(lon, lat), index(lon, lat ^ 1)))
            other = lat + 1 if lat % 2 else lat - 1
            if other == lat_count:
                second.append((index(lon, lat), index(lon_count - 1 - lon, lat)))
            elif other >= 0:
                second.append((index(lon, lat), index(lon, other)))
    return first, second


def lon_pairs(lon_count):
    first = [(lon, lon ^ 1) for lon in range(lon_count)]
    second = [(lon, (lon + 1 if lon % 2 else lon - 1) % lon_count) for lon in range(lon_count)]
    return first, second


def per_device(
    direction, residual, eof_basis, kappa_east, kappa_north, wet_mask, obs_base, obs_frac, obs_rinv
):
    levels = direction.shape[0]
    shape = functools.partial(jax.ShapeDtypeStruct, dtype=jnp.float32)
    local = functools.partial(pltpu.VMEM, dtype=jnp.float32)
    lon_count, lat_count = lax.axis_size("lon"), lax.axis_size("lat")
    lon, lat = lax.axis_index("lon"), lax.axis_index("lat")
    flags = jnp.stack([1 - lat % 2, 1 - lon % 2, (lat == lat_count - 1).astype(jnp.int32)])
    flags = flags.astype(jnp.int32)
    inputs = (
        direction,
        eof_basis,
        kappa_east,
        kappa_north,
        wet_mask,
        obs_base.reshape(1, -1),
        obs_frac.reshape(2, 1, -1),
        obs_rinv.reshape(levels, 1, -1),
    )
    own = pl.pallas_call(
        pack_tile,
        out_shape=local((ROWS + 2, PAD, LANES)),
        in_specs=[pl.BlockSpec(memory_space=pltpu.HBM)] * len(inputs),
        out_specs=VMEM,
        scratch_shapes=[pltpu.VMEM(x.shape, x.dtype) for x in inputs]
        + [pltpu.SemaphoreType.DMA((len(inputs),))],
        compiler_params=grant(8),
    )(*(pltpu.with_memory_space_constraint(x, pltpu.HBM) for x in inputs))
    direction, residual = near(direction), near(residual)
    first, second = lat_pairs(lon_count, lat_count)
    lat_b = lax.ppermute(own, ("lon", "lat"), second)
    lat_a = lax.ppermute(own, ("lon", "lat"), first)
    own, lat_a, lat_b = near(own), near(lat_a), near(lat_b)
    north_south, to_a, to_b = pl.pallas_call(
        pack_columns,
        out_shape=(local((2, ROWS + 2, PAD, LANES)), local((8, PAD, LANES)), local((8, PAD, LANES))),
        in_specs=[SMEM] + [VMEM] * 3,
        out_specs=(VMEM,) * 3,
        compiler_params=grant(8),
    )(flags, own, lat_a, lat_b)
    first, second = lon_pairs(lon_count)
    lon_b = lax.ppermute(to_b, "lon", second)
    lon_a = lax.ppermute(to_a, "lon", first)
    image, part = pl.pallas_call(
        local_image,
        out_shape=(local(direction.shape), local((lon_count, LANES))),
        in_specs=[SMEM] + [VMEM] * 7,
        out_specs=(VMEM,) * 2,
        compiler_params=grant(28),
        scratch_shapes=[
            pltpu.VMEM((BAND, PAD, 2 * LANES), jnp.float32),
            pltpu.VMEM((BAND, PAD, 2 * LANES), jnp.float32),
            pltpu.VMEM((BAND, PAD, 2 * LANES), jnp.float32),
            pltpu.VMEM((5, BAND, 2 * LANES), jnp.float32),
            pltpu.VMEM((3, 3, PAD, 2 * LANES), jnp.float32),
        ],
    )(flags, own, near(north_south), near(lon_a), near(lon_b), direction, residual, near(eof_basis.T))
    part = lax.all_to_all(part, "lon", 0, 0, tiled=True)
    part = jnp.broadcast_to(jnp.sum(part, axis=0, keepdims=True), (lat_count, LANES))
    part = lax.all_to_all(part, "lat", 0, 0, tiled=True)
    new_residual, new_direction, step_length = pl.pallas_call(
        finish,
        out_shape=(shape(direction.shape), shape(direction.shape), shape((1, 1))),
        in_specs=[VMEM] * 4,
        out_specs=(VMEM,) * 3,
        compiler_params=grant(8),
    )(near(part), near(image), residual, direction)
    return new_residual, new_direction, step_length.reshape(())


def solution(mesh):
    return jax.shard_map(
        per_device,
        mesh=mesh,
        in_specs=(
            P(None, "lat", "lon"),
            P(None, "lat", "lon"),
            P(),
            P("lat", "lon"),
            P("lat", "lon"),
            P("lat", "lon"),
            P("lat", "lon", None),
            P(None, "lat", "lon", None),
            P(None, "lat", "lon", None),
        ),
        out_specs=(P(None, "lat", "lon"), P(None, "lat", "lon"), P()),
        check_vma=False,
    )
```

```python
import functools

import jax
import jax.numpy as jnp
from jax import lax
from jax.experimental import pallas as pl
from jax.experimental.pallas import tpu as pltpu
from jax.sharding import PartitionSpec as P


HIGHEST = lax.Precision.HIGHEST
LANES = 128
ROWS = 8
PAD = 80
BAND = 3 * ROWS
HALO = 7
SLOTS = 12
SOUTH, OWN, NORTH = 0, 1, 2
EDGE, EDGE_ROW = 16, 4

SMEM = pl.BlockSpec(memory_space=pltpu.SMEM)
VMEM = pl.BlockSpec(memory_space=pltpu.VMEM)


def grant(mebibytes):
    return pltpu.CompilerParams(vmem_limit_bytes=mebibytes << 20)


def near(x):
    return pltpu.with_memory_space_constraint(x, pltpu.VMEM)


def split(x):
    high = x.astype(jnp.bfloat16)
    return high, (x - high.astype(jnp.float32)).astype(jnp.bfloat16)


def dot3(left, right, dims):
    (lh, ll), (rh, rl) = left, right
    mul = functools.partial(
        lax.dot_general, dimension_numbers=(dims, ((), ())), preferred_element_type=jnp.float32
    )
    return mul(lh, rh) + (mul(lh, rl) + mul(ll, rh))


def pack_tile(*refs):
    count = (len(refs) - 2) // 2
    sources, out_ref, held, sems = refs[:count], refs[count], refs[count + 1 : -1], refs[-1]
    copies = [
        pltpu.make_async_copy(source, target, sems.at[k])
        for k, (source, target) in enumerate(zip(sources, held))
    ]
    for copy in copies:
        copy.start()
    for copy in copies:
        copy.wait()
    dir_ref, eof_ref, ke_ref, kn_ref, wet_ref, base_ref, frac_ref, rinv_ref = held
    levels = dir_ref.shape[0]
    zeros = jnp.zeros((PAD - levels - 3, LANES), jnp.float32)
    eof = eof_ref[...]
    for row in range(ROWS):
        out_ref[row, :levels, :] = jnp.dot(
            eof, dir_ref[:, row, :], precision=HIGHEST, preferred_element_type=jnp.float32
        )
        out_ref[row, levels : levels + 1, :] = ke_ref[row : row + 1, :]
        out_ref[row, levels + 1 : levels + 2, :] = kn_ref[row : row + 1, :]
        out_ref[row, levels + 2 : levels + 3, :] = wet_ref[row : row + 1, :].astype(jnp.float32)
        out_ref[row, levels + 3 :, :] = zeros
    for half in range(2):
        cut = slice(half * LANES, (half + 1) * LANES)
        for level in range(levels):
            out_ref[ROWS + half, level : level + 1, :] = rinv_ref[level, :, cut]
        out_ref[ROWS + half, levels : levels + 1, :] = base_ref[:, cut].astype(jnp.float32)
        out_ref[ROWS + half, levels + 1 : levels + 2, :] = frac_ref[0, :, cut]
        out_ref[ROWS + half, levels + 2 : levels + 3, :] = frac_ref[1, :, cut]
        out_ref[ROWS + half, levels + 3 :, :] = zeros


def pack_columns(flags, own_ref, ra_ref, rb_ref, ns_ref, pa_ref, pb_ref):
    lat_even, lon_even, is_top = flags[0] == 1, flags[1] == 1, flags[2] == 1

    @pl.when(lat_even)
    def _():
        ns_ref[0] = ra_ref[...]
        ns_ref[1] = rb_ref[...]

    @pl.when(jnp.logical_not(lat_even))
    def _():
        ns_ref[0] = rb_ref[...]
        ns_ref[1] = ra_ref[...]

    @pl.when(is_top)
    def _():
        first = lax.broadcasted_iota(jnp.int32, (LANES, LANES), 0)
        second = lax.broadcasted_iota(jnp.int32, (LANES, LANES), 1)
        flip = jnp.where(first + second == LANES - 1, 1.0, 0.0).astype(jnp.float32)
        for row in range(ROWS):
            ns_ref[0, row] = jnp.dot(
                rb_ref[ROWS - 1 - row], flip, precision=HIGHEST, preferred_element_type=jnp.float32
            )

    lane = lax.broadcasted_iota(jnp.int32, (8, LANES), 1)

    def one(step, _):
        cut = pl.ds(pl.multiple_of(step * 8, 8), 8)
        for group in range(2):
            west = jnp.zeros((8, LANES), jnp.float32)
            east = jnp.zeros((8, LANES), jnp.float32)
            for slot in range(SLOTS):
                index = group * SLOTS + slot
                if index < ROWS:
                    tile = ns_ref[1, index, cut, :]
                elif index < 2 * ROWS:
                    tile = own_ref[index - ROWS, cut, :]
                else:
                    tile = ns_ref[0, index - 2 * ROWS, cut, :]
                start = HALO * slot
                here = (lane >= start) & (lane < start + HALO)
                west = jnp.where(here, pltpu.roll(tile, start, 1) if start else tile, west)
                east = jnp.where(here, pltpu.roll(tile, (start + HALO) % LANES, 1), east)
            pa_ref[group, cut, :] = jnp.where(lon_even, east, west)
            pb_ref[group, cut, :] = jnp.where(lon_even, west, east)
        return 0

    lax.fori_loop(0, PAD // 8, one, 0)
    for half in range(2):
        for ref in (pa_ref, pb_ref):
            ref[2 + 2 * SOUTH + half] = ns_ref[1, ROWS + half]
            ref[2 + 2 * OWN + half] = own_ref[ROWS + half]
            ref[2 + 2 * NORTH + half] = ns_ref[0, ROWS + half]


def diffuse_row(src, dst, coef, index):
    centre = src[index]
    width = centre.shape[1]
    wide = lambda k: jnp.broadcast_to(coef[k, pl.ds(index, 1), :], centre.shape)
    out = centre * wide(0)
    out = out + wide(1) * pltpu.roll(centre, width - 1, 1)
    out = out + wide(2) * pltpu.roll(centre, 1, 1)
    out = out + wide(3) * src[index + 1]
    out = out + wide(4) * src[index - 1]
    dst[index] = out


def diffuse_all(one, two, coef, low, high):
    for src, dst, trim in ((one, two, 0), (two, one, 1), (one, two, 2)):
        for index in range(low + trim, high - trim):
            diffuse_row(src, dst, coef, index)


def local_image(
    flags,
    own_ref,
    ns_ref,
    qa_ref,
    qb_ref,
    dir_ref,
    res_ref,
    eoft_ref,
    img_ref,
    part_ref,
    field,
    other,
    adj,
    coef,
    obs,
):
    lon_even, is_top = flags[1] == 1, flags[2] == 1
    levels = dir_ref.shape[0]
    width = 2 * LANES
    lane = lax.broadcasted_iota(jnp.int32, (8, LANES), 1)

    def unpack(step, _):
        cut = pl.ds(pl.multiple_of(step * 8, 8), 8)
        for group in range(2):
            first, second = qa_ref[group, cut, :], qb_ref[group, cut, :]
            east = jnp.where(lon_even, first, second)
            west = jnp.where(lon_even, second, first)
            for slot in range(SLOTS):
                index = group * SLOTS + slot
                if index < ROWS:
                    tile = ns_ref[1, index, cut, :]
                elif index < 2 * ROWS:
                    tile = own_ref[index - ROWS, cut, :]
                else:
                    tile = ns_ref[0, index - 2 * ROWS, cut, :]
                start = HALO * slot
                from_east = pltpu.roll(east, (LANES - start) % LANES, 1) if start else east
                from_west = pltpu.roll(west, (LANES - HALO - start) % LANES, 1)
                halo = jnp.where(
                    lane < HALO, from_east, jnp.where(lane >= LANES - HALO, from_west, 0.0)
                )
                field[index, cut, :LANES] = tile
                field[index, cut, LANES:] = halo
        return 0

    lax.fori_loop(0, PAD // 8, unpack, 0)

    ke, kn, wet = field[:, levels, :], field[:, levels + 1, :], field[:, levels + 2, :]
    row = lax.broadcasted_iota(jnp.int32, (BAND, width), 0)
    up = lambda x: jnp.concatenate([x[1:], x[:1]], 0)
    down = lambda x: jnp.concatenate([x[-1:], x[:-1]], 0)
    right = lambda x: pltpu.roll(x, width - 1, 1)
    left = lambda x: pltpu.roll(x, 1, 1)
    seam = 2 * ROWS - 1
    top = jnp.where(is_top, 1, 0)
    ke = jnp.where((row > seam) & (top == 1), right(ke), ke)
    kn_up = up(kn)
    kn = jnp.where(
        top == 1, jnp.where(row > seam, kn_up, jnp.where(row == seam, 0.5 * (kn + kn_up), kn)), kn
    )
    east_face = ke * wet * right(wet)
    north_face = kn * wet * up(wet)
    west_face, south_face = left(east_face), down(north_face)
    coef[0] = 1.0 - east_face - west_face - north_face - south_face
    coef[1] = east_face
    coef[2] = west_face
    coef[3] = north_face
    coef[4] = south_face

    diffuse_all(field, other, coef, 2, BAND - 2)
    physical = other

    for band in range(3):
        for half in range(2):
            cut = slice(half * LANES, (half + 1) * LANES)
            slot = 2 + 2 * band + half
            first, second = qa_ref[slot], qb_ref[slot]
            mid = (ns_ref[1, ROWS + half], own_ref[ROWS + half], ns_ref[0, ROWS + half])[band]
            obs[0, band, :, cut] = jnp.where(lon_even, second, first)
            obs[1, band, :, cut] = jnp.where(lon_even, first, second)
            obs[2, band, :, cut] = mid
    adj[...] = jnp.zeros(adj.shape, jnp.float32)
    cells = lax.broadcasted_iota(jnp.int32, (width, width), 0)
    keep = lax.broadcasted_iota(jnp.int32, (PAD, width), 0) < levels

    def places(side, band):
        base = obs[side, band, levels : levels + 1, :].astype(jnp.int32)
        p = obs[side, band, levels + 1 : levels + 2, :]
        q = obs[side, band, levels + 2 : levels + 3, :]
        j, i = base >> 7, base & (LANES - 1)
        turned = (top if band == NORTH else 0 * top) == 1
        rows = jnp.where(turned, 22 - j, j + ROWS * band)
        cols = jnp.where(turned, 126 - i, i)
        a0, a1 = jnp.where(turned, p, 1.0 - p), jnp.where(turned, 1.0 - p, p)
        b0, b1 = jnp.where(turned, q, 1.0 - q), jnp.where(turned, 1.0 - q, q)
        return rows, cols, a0, a1, b0, b1

    def weigh(side, band, profile):
        return jnp.where(keep, obs[side, band] * profile, 0.0)

    place = lax.broadcasted_iota(jnp.int32, (PAD, width), 1)
    packed = jnp.zeros((PAD, width), jnp.float32)
    for k in range(EDGE):
        cell = physical[EDGE_ROW + k]
        west = pltpu.roll(cell, (EDGE * k + 4) % width, 1)
        east = pltpu.roll(cell, (EDGE * k + 140) % width, 1)
        packed = jnp.where(
            (place >= EDGE * k) & (place < EDGE * k + 8),
            west,
            jnp.where((place >= EDGE * k + 8) & (place < EDGE * k + EDGE), east, packed),
        )
    packed = split(packed)
    edge_row, edge_col = cells >> 4, cells & (EDGE - 1)

    def beside(step, total):
        side, band = step & 1, step >> 1
        rows, cols, a0, a1, b0, b1 = places(side, band)
        rows = rows - EDGE_ROW
        cols = cols + jnp.where(side == 0, -124, 12)
        row_weight = jnp.where(edge_row == rows, a0, jnp.where(edge_row == rows + 1, a1, 0.0))
        col_weight = jnp.where(edge_col == cols, b0, jnp.where(edge_col == cols + 1, b1, 0.0))
        rhs = split(row_weight * col_weight)
        weighted = weigh(side, band, dot3(packed, rhs, ((1,), (0,))))
        return total + dot3(split(weighted), rhs, ((1,), (1,)))

    total = jnp.zeros((PAD, width), jnp.float32)
    for step in range(6):
        total = beside(step, total)
    for k in range(1, EDGE - 1):
        west = pltpu.roll(total, (width - EDGE * k - 4) % width, 1)
        east = pltpu.roll(total, (2 * width - EDGE * k - 140) % width, 1)
        adj[EDGE_ROW + k] = jnp.where(
            (place < 4) | (place >= width - 4),
            west,
            jnp.where((place >= 124) & (place < 132), east, 0.0),
        )

    for band, (begin, stop, lo, hi) in enumerate(((4, 9, 5, 9), (8, 17, 8, 17), (16, 20, 16, 19))):
        lhs = split(physical[begin:stop].reshape((stop - begin) * PAD, width))
        rows, cols, a0, a1, b0, b1 = places(2, band)
        lane0 = cols & (width - 1)
        lane1 = (cols + 1) & (width - 1)
        rhs = split(jnp.where(cells == lane0, b0, jnp.where(cells == lane1, b1, 0.0)))
        taken = dot3(lhs, rhs, ((1,), (0,)))
        row_weight = [
            jnp.where(rows == r, a0, jnp.where(rows == r - 1, a1, 0.0)) for r in range(begin, stop)
        ]
        profile = jnp.zeros((PAD, width), jnp.float32)
        for k in range(stop - begin):
            profile = profile + row_weight[k] * taken[k * PAD : (k + 1) * PAD]
        weighted = weigh(2, band, profile)
        spread = jnp.concatenate([row_weight[r - begin] * weighted for r in range(lo, hi)], 0)
        added = dot3(split(spread), rhs, ((1,), (1,)))
        adj[lo:hi] += added.reshape(hi - lo, PAD, width)

    diffuse_all(adj, other, coef, 6, BAND - 6)

    eoft = eoft_ref[...]
    rr = dim = rim = imim = jnp.zeros((levels, LANES), jnp.float32)
    for r in range(ROWS):
        back = jnp.dot(
            eoft, other[ROWS + r, :levels, :LANES], precision=HIGHEST, preferred_element_type=jnp.float32
        )
        d, res = dir_ref[:, r, :], res_ref[:, r, :]
        image = d + back
        img_ref[:, r, :] = image
        rr, dim, rim, imim = rr + res * res, dim + d * image, rim + res * image, imim + image * image
    lane = lax.broadcasted_iota(jnp.int32, part_ref.shape, 1)
    out = jnp.zeros(part_ref.shape, jnp.float32)
    for k, value in enumerate((rr, dim, rim, imim)):
        out = jnp.where(lane == k, jnp.sum(value), out)
    part_ref[...] = out


def finish(part_ref, img_ref, res_ref, dir_ref, new_res_ref, new_dir_ref, step_ref):
    total = jnp.sum(part_ref[...], axis=0, keepdims=True)
    lane = lax.broadcasted_iota(jnp.int32, total.shape, 1)
    rr, dim, rim, imim = (
        jnp.sum(jnp.where(lane == k, total, 0.0), axis=1, keepdims=True) for k in range(4)
    )
    step = rr / dim
    new_norm = rr + step * (step * imim - 2.0 * rim)
    beta = new_norm / rr
    step_ref[...] = step
    new_res = res_ref[...] - step[None] * img_ref[...]
    new_res_ref[...] = new_res
    new_dir_ref[...] = new_res + beta[None] * dir_ref[...]


def lat_pairs(lon_count, lat_count):
    index = lambda lon, lat: lon * lat_count + lat
    first, second = [], []
    for lon in range(lon_count):
        for lat in range(lat_count):
            first.append((index(lon, lat), index(lon, lat ^ 1)))
            other = lat + 1 if lat % 2 else lat - 1
            if other == lat_count:
                second.append((index(lon, lat), index(lon_count - 1 - lon, lat)))
            elif other >= 0:
                second.append((index(lon, lat), index(lon, other)))
    return first, second


def lon_pairs(lon_count):
    first = [(lon, lon ^ 1) for lon in range(lon_count)]
    second = [(lon, (lon + 1 if lon % 2 else lon - 1) % lon_count) for lon in range(lon_count)]
    return first, second


def per_device(
    direction, residual, eof_basis, kappa_east, kappa_north, wet_mask, obs_base, obs_frac, obs_rinv
):
    levels = direction.shape[0]
    shape = functools.partial(jax.ShapeDtypeStruct, dtype=jnp.float32)
    local = functools.partial(pltpu.VMEM, dtype=jnp.float32)
    lon_count, lat_count = lax.axis_size("lon"), lax.axis_size("lat")
    lon, lat = lax.axis_index("lon"), lax.axis_index("lat")
    flags = jnp.stack([1 - lat % 2, 1 - lon % 2, (lat == lat_count - 1).astype(jnp.int32)])
    flags = flags.astype(jnp.int32)
    inputs = (
        direction,
        eof_basis,
        kappa_east,
        kappa_north,
        wet_mask,
        obs_base.reshape(1, -1),
        obs_frac.reshape(2, 1, -1),
        obs_rinv.reshape(levels, 1, -1),
    )
    own = pl.pallas_call(
        pack_tile,
        out_shape=local((ROWS + 2, PAD, LANES)),
        in_specs=[pl.BlockSpec(memory_space=pltpu.HBM)] * len(inputs),
        out_specs=VMEM,
        scratch_shapes=[pltpu.VMEM(x.shape, x.dtype) for x in inputs]
        + [pltpu.SemaphoreType.DMA((len(inputs),))],
        compiler_params=grant(8),
    )(*(pltpu.with_memory_space_constraint(x, pltpu.HBM) for x in inputs))
    direction, residual = near(direction), near(residual)
    first, second = lat_pairs(lon_count, lat_count)
    lat_b = lax.ppermute(own, ("lon", "lat"), second)
    lat_a = lax.ppermute(own, ("lon", "lat"), first)
    own, lat_a, lat_b = near(own), near(lat_a), near(lat_b)
    north_south, to_a, to_b = pl.pallas_call(
        pack_columns,
        out_shape=(local((2, ROWS + 2, PAD, LANES)), local((8, PAD, LANES)), local((8, PAD, LANES))),
        in_specs=[SMEM] + [VMEM] * 3,
        out_specs=(VMEM,) * 3,
        compiler_params=grant(8),
    )(flags, own, lat_a, lat_b)
    first, second = lon_pairs(lon_count)
    lon_b = lax.ppermute(to_b, "lon", second)
    lon_a = lax.ppermute(to_a, "lon", first)
    image, part = pl.pallas_call(
        local_image,
        out_shape=(local(direction.shape), local((lon_count, LANES))),
        in_specs=[SMEM] + [VMEM] * 7,
        out_specs=(VMEM,) * 2,
        compiler_params=grant(28),
        scratch_shapes=[
            pltpu.VMEM((BAND, PAD, 2 * LANES), jnp.float32),
            pltpu.VMEM((BAND, PAD, 2 * LANES), jnp.float32),
            pltpu.VMEM((BAND, PAD, 2 * LANES), jnp.float32),
            pltpu.VMEM((5, BAND, 2 * LANES), jnp.float32),
            pltpu.VMEM((3, 3, PAD, 2 * LANES), jnp.float32),
        ],
    )(flags, own, near(north_south), near(lon_a), near(lon_b), direction, residual, near(eof_basis.T))
    part = lax.all_to_all(part, "lon", 0, 0, tiled=True)
    part = jnp.broadcast_to(jnp.sum(part, axis=0, keepdims=True), (lat_count, LANES))
    part = lax.all_to_all(part, "lat", 0, 0, tiled=True)
    new_residual, new_direction, step_length = pl.pallas_call(
        finish,
        out_shape=(shape(direction.shape), shape(direction.shape), shape((1, 1))),
        in_specs=[VMEM] * 4,
        out_specs=(VMEM,) * 3,
        compiler_params=grant(8),
    )(near(part), near(image), residual, direction)
    return new_residual, new_direction, step_length.reshape(())


def solution(mesh):
    return jax.shard_map(
        per_device,
        mesh=mesh,
        in_specs=(
            P(None, "lat", "lon"),
            P(None, "lat", "lon"),
            P(),
            P("lat", "lon"),
            P("lat", "lon"),
            P("lat", "lon"),
            P("lat", "lon", None),
            P(None, "lat", "lon", None),
            P(None, "lat", "lon", None),
        ),
        out_specs=(P(None, "lat", "lon"), P(None, "lat", "lon"), P()),
        check_vma=False,
    )
```

```python
import functools

import jax
import jax.numpy as jnp
from jax import lax
from jax.experimental import pallas as pl
from jax.experimental.pallas import tpu as pltpu
from jax.sharding import PartitionSpec as P


HIGHEST = lax.Precision.HIGHEST
LANES = 128
ROWS = 8
PAD = 80
BAND = 3 * ROWS
HALO = 7
SLOTS = 12
SOUTH, OWN, NORTH = 0, 1, 2
EDGE, EDGE_ROW = 16, 4

SMEM = pl.BlockSpec(memory_space=pltpu.SMEM)
VMEM = pl.BlockSpec(memory_space=pltpu.VMEM)


def grant(mebibytes):
    return pltpu.CompilerParams(vmem_limit_bytes=mebibytes << 20)


def near(x):
    return pltpu.with_memory_space_constraint(x, pltpu.VMEM)


def split(x):
    high = x.astype(jnp.bfloat16)
    return high, (x - high.astype(jnp.float32)).astype(jnp.bfloat16)


def dot3(left, right, dims):
    (lh, ll), (rh, rl) = left, right
    mul = functools.partial(
        lax.dot_general, dimension_numbers=(dims, ((), ())), preferred_element_type=jnp.float32
    )
    return mul(lh, rh) + (mul(lh, rl) + mul(ll, rh))


def pack_tile(*refs):
    count = (len(refs) - 4) // 2
    sources, held, sems = refs[:count], refs[count + 3 : -1], refs[-1]
    out_ref, far_ref, near_ref = refs[count : count + 3]
    copies = [
        pltpu.make_async_copy(source, target, sems.at[k])
        for k, (source, target) in enumerate(zip(sources, held))
    ]
    for copy in copies:
        copy.start()
    for copy in copies:
        copy.wait()
    dir_ref, eof_ref, ke_ref, kn_ref, wet_ref, base_ref, frac_ref, rinv_ref = held
    levels = dir_ref.shape[0]
    zeros = jnp.zeros((PAD - levels - 3, LANES), jnp.float32)
    eof = eof_ref[...]
    for row in range(ROWS):
        out_ref[row, :levels, :] = jnp.dot(
            eof, dir_ref[:, row, :], precision=HIGHEST, preferred_element_type=jnp.float32
        )
        out_ref[row, levels : levels + 1, :] = ke_ref[row : row + 1, :]
        out_ref[row, levels + 1 : levels + 2, :] = kn_ref[row : row + 1, :]
        out_ref[row, levels + 2 : levels + 3, :] = wet_ref[row : row + 1, :].astype(jnp.float32)
        out_ref[row, levels + 3 :, :] = zeros
    for half in range(2):
        cut = slice(half * LANES, (half + 1) * LANES)
        for level in range(levels):
            out_ref[ROWS + half, level : level + 1, :] = rinv_ref[level, :, cut]
        out_ref[ROWS + half, levels : levels + 1, :] = base_ref[:, cut].astype(jnp.float32)
        out_ref[ROWS + half, levels + 1 : levels + 2, :] = frac_ref[0, :, cut]
        out_ref[ROWS + half, levels + 2 : levels + 3, :] = frac_ref[1, :, cut]
        out_ref[ROWS + half, levels + 3 :, :] = zeros
        far_ref[HALO + half] = out_ref[ROWS + half]
        near_ref[HALO + half] = out_ref[ROWS + half]
    northern = lax.axis_index("lat") % 2 == 1
    for row in range(HALO):
        low, high = out_ref[row], out_ref[row + 1]
        far_ref[row] = jnp.where(northern, high, low)
        near_ref[row] = jnp.where(northern, low, high)


def row_tile(own_ref, ns_ref, index):
    if index in (0, BAND - 1):
        return None
    if index < ROWS:
        return ns_ref[1, index - 1]
    return own_ref[index - ROWS] if index < 2 * ROWS else ns_ref[0, index - 2 * ROWS]


def pack_columns(flags, own_ref, ra_ref, rb_ref, ns_ref, pa_ref, pb_ref):
    lat_even, lon_even, is_top = flags[0] == 1, flags[1] == 1, flags[2] == 1

    @pl.when(lat_even)
    def _():
        ns_ref[0] = ra_ref[...]
        ns_ref[1] = rb_ref[...]

    @pl.when(jnp.logical_not(lat_even))
    def _():
        ns_ref[0] = rb_ref[...]
        ns_ref[1] = ra_ref[...]

    @pl.when(is_top)
    def _():
        first = lax.broadcasted_iota(jnp.int32, (LANES, LANES), 0)
        second = lax.broadcasted_iota(jnp.int32, (LANES, LANES), 1)
        flip = jnp.where(first + second == LANES - 1, 1.0, 0.0).astype(jnp.float32)
        for row in range(HALO):
            ns_ref[0, row] = jnp.dot(
                rb_ref[HALO - 1 - row], flip, precision=HIGHEST, preferred_element_type=jnp.float32
            )

    lane = lax.broadcasted_iota(jnp.int32, (PAD, LANES), 1)
    for group in range(2):
        west = jnp.zeros((PAD, LANES), jnp.float32)
        east = jnp.zeros((PAD, LANES), jnp.float32)
        for slot in range(SLOTS):
            tile = row_tile(own_ref, ns_ref, group * SLOTS + slot)
            if tile is None:
                continue
            start = HALO * slot
            here = (lane >= start) & (lane < start + HALO)
            west = jnp.where(here, pltpu.roll(tile, start, 1) if start else tile, west)
            east = jnp.where(here, pltpu.roll(tile, (start + HALO) % LANES, 1), east)
        pa_ref[group] = jnp.where(lon_even, east, west)
        pb_ref[group] = jnp.where(lon_even, west, east)
    for half in range(2):
        for ref in (pa_ref, pb_ref):
            ref[2 + 2 * SOUTH + half] = ns_ref[1, HALO + half]
            ref[2 + 2 * OWN + half] = own_ref[ROWS + half]
            ref[2 + 2 * NORTH + half] = ns_ref[0, HALO + half]


def diffuse_row(src, dst, coef, index):
    centre = src[index]
    width = centre.shape[1]
    wide = lambda k: jnp.broadcast_to(coef[k, pl.ds(index, 1), :], centre.shape)
    out = centre * wide(0)
    out = out + wide(1) * pltpu.roll(centre, width - 1, 1)
    out = out + wide(2) * pltpu.roll(centre, 1, 1)
    out = out + wide(3) * src[index + 1]
    out = out + wide(4) * src[index - 1]
    dst[index] = out


def diffuse_all(one, two, coef, low, high):
    for src, dst, trim in ((one, two, 0), (two, one, 1), (one, two, 2)):
        for index in range(low + trim, high - trim):
            diffuse_row(src, dst, coef, index)


def local_image(
    flags,
    own_ref,
    ns_ref,
    qa_ref,
    qb_ref,
    dir_ref,
    res_ref,
    eoft_ref,
    img_ref,
    part_ref,
    field,
    other,
    adj,
    coef,
    obs,
):
    lon_even, is_top = flags[1] == 1, flags[2] == 1
    levels = dir_ref.shape[0]
    width = 2 * LANES
    lane = lax.broadcasted_iota(jnp.int32, (PAD, LANES), 1)
    for group in range(2):
        first, second = qa_ref[group], qb_ref[group]
        east = jnp.where(lon_even, first, second)
        west = jnp.where(lon_even, second, first)
        for slot in range(SLOTS):
            index = group * SLOTS + slot
            tile = row_tile(own_ref, ns_ref, index)
            if tile is None:
                field[index] = jnp.zeros((PAD, width), jnp.float32)
                continue
            start = HALO * slot
            from_east = pltpu.roll(east, (LANES - start) % LANES, 1) if start else east
            from_west = pltpu.roll(west, (LANES - HALO - start) % LANES, 1)
            field[index, :, :LANES] = tile
            field[index, :, LANES:] = jnp.where(
                lane < HALO, from_east, jnp.where(lane >= LANES - HALO, from_west, 0.0)
            )

    ke, kn, wet = field[:, levels, :], field[:, levels + 1, :], field[:, levels + 2, :]
    row = lax.broadcasted_iota(jnp.int32, (BAND, width), 0)
    up = lambda x: jnp.concatenate([x[1:], x[:1]], 0)
    down = lambda x: jnp.concatenate([x[-1:], x[:-1]], 0)
    right = lambda x: pltpu.roll(x, width - 1, 1)
    left = lambda x: pltpu.roll(x, 1, 1)
    seam = 2 * ROWS - 1
    top = jnp.where(is_top, 1, 0)
    ke = jnp.where((row > seam) & (top == 1), right(ke), ke)
    kn_up = up(kn)
    kn = jnp.where(
        top == 1, jnp.where(row > seam, kn_up, jnp.where(row == seam, 0.5 * (kn + kn_up), kn)), kn
    )
    east_face = ke * wet * right(wet)
    north_face = kn * wet * up(wet)
    west_face, south_face = left(east_face), down(north_face)
    coef[0] = 1.0 - east_face - west_face - north_face - south_face
    coef[1] = east_face
    coef[2] = west_face
    coef[3] = north_face
    coef[4] = south_face

    diffuse_all(field, other, coef, 2, BAND - 2)
    physical = other

    for band in range(3):
        for half in range(2):
            cut = slice(half * LANES, (half + 1) * LANES)
            slot = 2 + 2 * band + half
            first, second = qa_ref[slot], qb_ref[slot]
            mid = (ns_ref[1, HALO + half], own_ref[ROWS + half], ns_ref[0, HALO + half])[band]
            obs[0, band, :, cut] = jnp.where(lon_even, second, first)
            obs[1, band, :, cut] = jnp.where(lon_even, first, second)
            obs[2, band, :, cut] = mid
    adj[...] = jnp.zeros(adj.shape, jnp.float32)
    cells = lax.broadcasted_iota(jnp.int32, (width, width), 0)
    keep = lax.broadcasted_iota(jnp.int32, (PAD, width), 0) < levels

    def places(side, band):
        base = obs[side, band, levels : levels + 1, :].astype(jnp.int32)
        p = obs[side, band, levels + 1 : levels + 2, :]
        q = obs[side, band, levels + 2 : levels + 3, :]
        j, i = base >> 7, base & (LANES - 1)
        turned = (top if band == NORTH else 0 * top) == 1
        rows = jnp.where(turned, 22 - j, j + ROWS * band)
        cols = jnp.where(turned, 126 - i, i)
        a0, a1 = jnp.where(turned, p, 1.0 - p), jnp.where(turned, 1.0 - p, p)
        b0, b1 = jnp.where(turned, q, 1.0 - q), jnp.where(turned, 1.0 - q, q)
        return rows, cols, a0, a1, b0, b1

    def weigh(side, band, profile):
        return jnp.where(keep, obs[side, band] * profile, 0.0)

    place = lax.broadcasted_iota(jnp.int32, (PAD, width), 1)
    packed = jnp.zeros((PAD, width), jnp.float32)
    for k in range(EDGE):
        cell = physical[EDGE_ROW + k]
        west = pltpu.roll(cell, (EDGE * k + 4) % width, 1)
        east = pltpu.roll(cell, (EDGE * k + 140) % width, 1)
        packed = jnp.where(
            (place >= EDGE * k) & (place < EDGE * k + 8),
            west,
            jnp.where((place >= EDGE * k + 8) & (place < EDGE * k + EDGE), east, packed),
        )
    packed = split(packed)
    edge_row, edge_col = cells >> 4, cells & (EDGE - 1)

    def beside(step, total):
        side, band = step & 1, step >> 1
        rows, cols, a0, a1, b0, b1 = places(side, band)
        rows = rows - EDGE_ROW
        cols = cols + jnp.where(side == 0, -124, 12)
        row_weight = jnp.where(edge_row == rows, a0, jnp.where(edge_row == rows + 1, a1, 0.0))
        col_weight = jnp.where(edge_col == cols, b0, jnp.where(edge_col == cols + 1, b1, 0.0))
        rhs = split(row_weight * col_weight)
        weighted = weigh(side, band, dot3(packed, rhs, ((1,), (0,))))
        return total + dot3(split(weighted), rhs, ((1,), (1,)))

    total = jnp.zeros((PAD, width), jnp.float32)
    for step in range(6):
        total = beside(step, total)
    for k in range(1, EDGE - 1):
        west = pltpu.roll(total, (width - EDGE * k - 4) % width, 1)
        east = pltpu.roll(total, (2 * width - EDGE * k - 140) % width, 1)
        adj[EDGE_ROW + k] = jnp.where(
            (place < 4) | (place >= width - 4),
            west,
            jnp.where((place >= 124) & (place < 132), east, 0.0),
        )

    for band, (begin, stop, lo, hi) in enumerate(((4, 9, 5, 9), (8, 17, 8, 17), (16, 20, 16, 19))):
        lhs = split(physical[begin:stop].reshape((stop - begin) * PAD, width))
        rows, cols, a0, a1, b0, b1 = places(2, band)
        lane0 = cols & (width - 1)
        lane1 = (cols + 1) & (width - 1)
        rhs = split(jnp.where(cells == lane0, b0, jnp.where(cells == lane1, b1, 0.0)))
        taken = dot3(lhs, rhs, ((1,), (0,)))
        row_weight = [
            jnp.where(rows == r, a0, jnp.where(rows == r - 1, a1, 0.0)) for r in range(begin, stop)
        ]
        profile = jnp.zeros((PAD, width), jnp.float32)
        for k in range(stop - begin):
            profile = profile + row_weight[k] * taken[k * PAD : (k + 1) * PAD]
        weighted = weigh(2, band, profile)
        spread = jnp.concatenate([row_weight[r - begin] * weighted for r in range(lo, hi)], 0)
        added = dot3(split(spread), rhs, ((1,), (1,)))
        adj[lo:hi] += added.reshape(hi - lo, PAD, width)

    diffuse_all(adj, other, coef, 6, BAND - 6)

    eoft = split(eoft_ref[...])
    rr = dim = rim = imim = jnp.zeros((levels, LANES), jnp.float32)
    for r in range(ROWS):
        back = dot3(eoft, split(other[ROWS + r, :levels, :LANES]), ((1,), (0,)))
        d, res = dir_ref[:, r, :], res_ref[:, r, :]
        image = d + back
        img_ref[:, r, :] = image
        rr, dim, rim, imim = rr + res * res, dim + d * image, rim + res * image, imim + image * image
    lane = lax.broadcasted_iota(jnp.int32, part_ref.shape, 1)
    out = jnp.zeros(part_ref.shape, jnp.float32)
    for k, value in enumerate((rr, dim, rim, imim)):
        out = jnp.where(lane == k, jnp.sum(value), out)
    part_ref[...] = out


def finish(part_ref, img_ref, res_ref, dir_ref, new_res_ref, new_dir_ref, step_ref):
    total = jnp.sum(part_ref[...], axis=0, keepdims=True)
    lane = lax.broadcasted_iota(jnp.int32, total.shape, 1)
    rr, dim, rim, imim = (
        jnp.sum(jnp.where(lane == k, total, 0.0), axis=1, keepdims=True) for k in range(4)
    )
    step = rr / dim
    new_norm = rr + step * (step * imim - 2.0 * rim)
    beta = new_norm / rr
    step_ref[...] = step
    new_res = res_ref[...] - step[None] * img_ref[...]
    new_res_ref[...] = new_res
    new_dir_ref[...] = new_res + beta[None] * dir_ref[...]


def lat_pairs(lon_count, lat_count):
    index = lambda lon, lat: lon * lat_count + lat
    first, second = [], []
    for lon in range(lon_count):
        for lat in range(lat_count):
            first.append((index(lon, lat), index(lon, lat ^ 1)))
            other = lat + 1 if lat % 2 else lat - 1
            if other == lat_count:
                second.append((index(lon, lat), index(lon_count - 1 - lon, lat)))
            elif other >= 0:
                second.append((index(lon, lat), index(lon, other)))
    return first, second


def lon_pairs(lon_count):
    first = [(lon, lon ^ 1) for lon in range(lon_count)]
    second = [(lon, (lon + 1 if lon % 2 else lon - 1) % lon_count) for lon in range(lon_count)]
    return first, second


def per_device(
    direction, residual, eof_basis, kappa_east, kappa_north, wet_mask, obs_base, obs_frac, obs_rinv
):
    levels = direction.shape[0]
    shape = functools.partial(jax.ShapeDtypeStruct, dtype=jnp.float32)
    local = functools.partial(pltpu.VMEM, dtype=jnp.float32)
    lon_count, lat_count = lax.axis_size("lon"), lax.axis_size("lat")
    lon, lat = lax.axis_index("lon"), lax.axis_index("lat")
    flags = jnp.stack([1 - lat % 2, 1 - lon % 2, (lat == lat_count - 1).astype(jnp.int32)])
    flags = flags.astype(jnp.int32)
    inputs = (
        direction,
        eof_basis,
        kappa_east,
        kappa_north,
        wet_mask,
        obs_base.reshape(1, -1),
        obs_frac.reshape(2, 1, -1),
        obs_rinv.reshape(levels, 1, -1),
    )
    own, far, close = pl.pallas_call(
        pack_tile,
        out_shape=(
            local((ROWS + 2, PAD, LANES)),
            local((HALO + 2, PAD, LANES)),
            local((HALO + 2, PAD, LANES)),
        ),
        in_specs=[pl.BlockSpec(memory_space=pltpu.HBM)] * len(inputs),
        out_specs=(VMEM,) * 3,
        scratch_shapes=[pltpu.VMEM(x.shape, x.dtype) for x in inputs]
        + [pltpu.SemaphoreType.DMA((len(inputs),))],
        compiler_params=grant(8),
    )(*(pltpu.with_memory_space_constraint(x, pltpu.HBM) for x in inputs))
    direction, residual = near(direction), near(residual)
    first, second = lat_pairs(lon_count, lat_count)
    lat_b = lax.ppermute(far, ("lon", "lat"), second)
    lat_a = lax.ppermute(close, ("lon", "lat"), first)
    own, lat_a, lat_b = near(own), near(lat_a), near(lat_b)
    north_south, to_a, to_b = pl.pallas_call(
        pack_columns,
        out_shape=(local((2, HALO + 2, PAD, LANES)), local((8, PAD, LANES)), local((8, PAD, LANES))),
        in_specs=[SMEM] + [VMEM] * 3,
        out_specs=(VMEM,) * 3,
        compiler_params=grant(8),
    )(flags, own, lat_a, lat_b)
    first, second = lon_pairs(lon_count)
    lon_b = lax.ppermute(to_b, "lon", second)
    lon_a = lax.ppermute(to_a, "lon", first)
    image, part = pl.pallas_call(
        local_image,
        out_shape=(local(direction.shape), local((lon_count, LANES))),
        in_specs=[SMEM] + [VMEM] * 7,
        out_specs=(VMEM,) * 2,
        compiler_params=grant(28),
        scratch_shapes=[
            pltpu.VMEM((BAND, PAD, 2 * LANES), jnp.float32),
            pltpu.VMEM((BAND, PAD, 2 * LANES), jnp.float32),
            pltpu.VMEM((BAND, PAD, 2 * LANES), jnp.float32),
            pltpu.VMEM((5, BAND, 2 * LANES), jnp.float32),
            pltpu.VMEM((3, 3, PAD, 2 * LANES), jnp.float32),
        ],
    )(flags, own, near(north_south), near(lon_a), near(lon_b), direction, residual, near(eof_basis.T))
    part = lax.all_to_all(part, "lon", 0, 0, tiled=True)
    part = jnp.broadcast_to(jnp.sum(part, axis=0, keepdims=True), (lat_count, LANES))
    part = lax.all_to_all(part, "lat", 0, 0, tiled=True)
    new_residual, new_direction, step_length = pl.pallas_call(
        finish,
        out_shape=(shape(direction.shape), shape(direction.shape), shape((1, 1))),
        in_specs=[VMEM] * 4,
        out_specs=(VMEM,) * 3,
        compiler_params=grant(8),
    )(near(part), near(image), residual, direction)
    return new_residual, new_direction, step_length.reshape(())


def solution(mesh):
    return jax.shard_map(
        per_device,
        mesh=mesh,
        in_specs=(
            P(None, "lat", "lon"),
            P(None, "lat", "lon"),
            P(),
            P("lat", "lon"),
            P("lat", "lon"),
            P("lat", "lon"),
            P("lat", "lon", None),
            P(None, "lat", "lon", None),
            P(None, "lat", "lon", None),
        ),
        out_specs=(P(None, "lat", "lon"), P(None, "lat", "lon"), P()),
        check_vma=False,
    )
```

```python
import functools

import jax
import jax.numpy as jnp
from jax import lax
from jax.experimental import pallas as pl
from jax.experimental.pallas import tpu as pltpu
from jax.sharding import PartitionSpec as P


HIGHEST = lax.Precision.HIGHEST
LANES = 128
ROWS = 8
PAD = 80
BAND = 3 * ROWS
HALO = 7
SLOTS = 12
SOUTH, OWN, NORTH = 0, 1, 2
EDGE, EDGE_ROW = 16, 4

SMEM = pl.BlockSpec(memory_space=pltpu.SMEM)
VMEM = pl.BlockSpec(memory_space=pltpu.VMEM)


def grant(mebibytes):
    return pltpu.CompilerParams(vmem_limit_bytes=mebibytes << 20)


def near(x):
    return pltpu.with_memory_space_constraint(x, pltpu.VMEM)


def split(x):
    high = x.astype(jnp.bfloat16)
    return high, (x - high.astype(jnp.float32)).astype(jnp.bfloat16)


def dot3(left, right, dims):
    (lh, ll), (rh, rl) = left, right
    mul = functools.partial(
        lax.dot_general, dimension_numbers=(dims, ((), ())), preferred_element_type=jnp.float32
    )
    return mul(lh, rh) + (mul(lh, rl) + mul(ll, rh))


def pack_tile(*refs):
    count = (len(refs) - 4) // 2
    sources, held, sems = refs[:count], refs[count + 3 : -1], refs[-1]
    out_ref, far_ref, near_ref = refs[count : count + 3]
    copies = [
        pltpu.make_async_copy(source, target, sems.at[k])
        for k, (source, target) in enumerate(zip(sources, held))
    ]
    for copy in copies:
        copy.start()
    for copy in copies:
        copy.wait()
    dir_ref, eof_ref, ke_ref, kn_ref, wet_ref, base_ref, frac_ref, rinv_ref = held
    levels = dir_ref.shape[0]
    zeros = jnp.zeros((PAD - levels - 3, LANES), jnp.float32)
    eof = eof_ref[...]
    for row in range(ROWS):
        out_ref[row, :levels, :] = jnp.dot(
            eof, dir_ref[:, row, :], precision=HIGHEST, preferred_element_type=jnp.float32
        )
        out_ref[row, levels : levels + 1, :] = ke_ref[row : row + 1, :]
        out_ref[row, levels + 1 : levels + 2, :] = kn_ref[row : row + 1, :]
        out_ref[row, levels + 2 : levels + 3, :] = wet_ref[row : row + 1, :].astype(jnp.float32)
        out_ref[row, levels + 3 :, :] = zeros
    for half in range(2):
        cut = slice(half * LANES, (half + 1) * LANES)
        for level in range(levels):
            out_ref[ROWS + half, level : level + 1, :] = rinv_ref[level, :, cut]
        out_ref[ROWS + half, levels : levels + 1, :] = base_ref[:, cut].astype(jnp.float32)
        out_ref[ROWS + half, levels + 1 : levels + 2, :] = frac_ref[0, :, cut]
        out_ref[ROWS + half, levels + 2 : levels + 3, :] = frac_ref[1, :, cut]
        out_ref[ROWS + half, levels + 3 :, :] = zeros
        far_ref[HALO + half] = out_ref[ROWS + half]
        near_ref[HALO + half] = out_ref[ROWS + half]
    northern = lax.axis_index("lat") % 2 == 1
    for row in range(HALO):
        low, high = out_ref[row], out_ref[row + 1]
        far_ref[row] = jnp.where(northern, high, low)
        near_ref[row] = jnp.where(northern, low, high)


def row_tile(own_ref, ns_ref, index, cut=slice(None)):
    if index in (0, BAND - 1):
        return None
    if index < ROWS:
        return ns_ref[1, index - 1, cut, :]
    return own_ref[index - ROWS, cut, :] if index < 2 * ROWS else ns_ref[0, index - 2 * ROWS, cut, :]


def pack_columns(flags, own_ref, ra_ref, rb_ref, ns_ref, pa_ref, pb_ref):
    lat_even, lon_even, is_top = flags[0] == 1, flags[1] == 1, flags[2] == 1

    @pl.when(lat_even)
    def _():
        ns_ref[0] = ra_ref[...]
        ns_ref[1] = rb_ref[...]

    @pl.when(jnp.logical_not(lat_even))
    def _():
        ns_ref[0] = rb_ref[...]
        ns_ref[1] = ra_ref[...]

    @pl.when(is_top)
    def _():
        first = lax.broadcasted_iota(jnp.int32, (LANES, LANES), 0)
        second = lax.broadcasted_iota(jnp.int32, (LANES, LANES), 1)
        flip = jnp.where(first + second == LANES - 1, 1.0, 0.0).astype(jnp.float32)
        for row in range(HALO):
            ns_ref[0, row] = jnp.dot(
                rb_ref[HALO - 1 - row], flip, precision=HIGHEST, preferred_element_type=jnp.float32
            )

    lane = lax.broadcasted_iota(jnp.int32, (PAD, LANES), 1)
    for group in range(2):
        west = jnp.zeros((PAD, LANES), jnp.float32)
        east = jnp.zeros((PAD, LANES), jnp.float32)
        for slot in range(SLOTS):
            tile = row_tile(own_ref, ns_ref, group * SLOTS + slot)
            if tile is None:
                continue
            start = HALO * slot
            here = (lane >= start) & (lane < start + HALO)
            west = jnp.where(here, pltpu.roll(tile, start, 1) if start else tile, west)
            east = jnp.where(here, pltpu.roll(tile, (start + HALO) % LANES, 1), east)
        pa_ref[group] = jnp.where(lon_even, east, west)
        pb_ref[group] = jnp.where(lon_even, west, east)
    for half in range(2):
        for ref in (pa_ref, pb_ref):
            ref[2 + 2 * SOUTH + half] = ns_ref[1, HALO + half]
            ref[2 + 2 * OWN + half] = own_ref[ROWS + half]
            ref[2 + 2 * NORTH + half] = ns_ref[0, HALO + half]


def diffuse_row(src, dst, coef, index):
    centre = src[index]
    width = centre.shape[1]
    wide = lambda k: jnp.broadcast_to(coef[k, pl.ds(index, 1), :], centre.shape)
    out = centre * wide(0)
    out = out + wide(1) * pltpu.roll(centre, width - 1, 1)
    out = out + wide(2) * pltpu.roll(centre, 1, 1)
    out = out + wide(3) * src[index + 1]
    out = out + wide(4) * src[index - 1]
    dst[index] = out


def diffuse_all(one, two, coef, low, high):
    for src, dst, trim in ((one, two, 0), (two, one, 1), (one, two, 2)):
        for index in range(low + trim, high - trim):
            diffuse_row(src, dst, coef, index)


def set_faces(coef, ke, kn, wet, top):
    width = ke.shape[1]
    row = lax.broadcasted_iota(jnp.int32, ke.shape, 0)
    up = lambda x: jnp.concatenate([x[1:], x[:1]], 0)
    down = lambda x: jnp.concatenate([x[-1:], x[:-1]], 0)
    right = lambda x: pltpu.roll(x, width - 1, 1)
    left = lambda x: pltpu.roll(x, 1, 1)
    seam = 2 * ROWS - 1
    ke = jnp.where((row > seam) & (top == 1), right(ke), ke)
    kn_up = up(kn)
    kn = jnp.where(
        top == 1, jnp.where(row > seam, kn_up, jnp.where(row == seam, 0.5 * (kn + kn_up), kn)), kn
    )
    east_face = ke * wet * right(wet)
    north_face = kn * wet * up(wet)
    west_face, south_face = left(east_face), down(north_face)
    coef[0] = 1.0 - east_face - west_face - north_face - south_face
    coef[1] = east_face
    coef[2] = west_face
    coef[3] = north_face
    coef[4] = south_face


def inner_tile(levels, flags, own_ref, ns_ref, out_ref, field, coef):
    for index in range(BAND):
        tile = row_tile(own_ref, ns_ref, index)
        field[index] = jnp.zeros((PAD, LANES), jnp.float32) if tile is None else tile
    ke, kn, wet = field[:, levels, :], field[:, levels + 1, :], field[:, levels + 2, :]
    set_faces(coef, ke, kn, wet, flags[2])
    diffuse_all(field, out_ref, coef, 2, BAND - 2)


def local_image(
    flags,
    own_ref,
    ns_ref,
    qa_ref,
    qb_ref,
    dir_ref,
    res_ref,
    eof_ref,
    inner_ref,
    img_ref,
    part_ref,
    strip,
    strip_next,
    masks,
    other,
    adj,
    coef,
    strip_coef,
    obs,
):
    lon_even, is_top = flags[1] == 1, flags[2] == 1
    levels = dir_ref.shape[0]
    width = 2 * LANES
    lane = lax.broadcasted_iota(jnp.int32, (PAD, LANES), 1)
    slab = slice(PAD - 8, PAD)
    half_turn = LANES // 2
    for group in range(2):
        first, second = qa_ref[group], qb_ref[group]
        east = jnp.where(lon_even, first, second)
        west = jnp.where(lon_even, second, first)
        for slot in range(SLOTS):
            index = group * SLOTS + slot
            tile = row_tile(own_ref, ns_ref, index)
            if tile is None:
                strip[index] = jnp.zeros((PAD, LANES), jnp.float32)
                masks[index] = jnp.zeros((8, width), jnp.float32)
                continue
            start = HALO * slot
            from_east = pltpu.roll(east, (half_turn + LANES - start) % LANES, 1)
            from_west = pltpu.roll(west, (LANES - HALO - start) % LANES, 1)
            turned = pltpu.roll(tile, half_turn, 1)
            line = jnp.where(lane >= LANES - HALO, from_west, 0.0)
            line = jnp.where((lane >= half_turn) & (lane < half_turn + HALO), from_east, line)
            line = jnp.where((lane >= half_turn - HALO) & (lane < half_turn), turned, line)
            strip[index] = jnp.where(lane < HALO, tile, line)
            masks[index, :, :LANES] = tile[slab]
            beyond = pltpu.roll(from_east[slab], half_turn, 1)
            masks[index, :, LANES:] = jnp.where(
                lane[slab] < HALO, beyond, jnp.where(lane[slab] >= LANES - HALO, from_west[slab], 0.0)
            )

    top = jnp.where(is_top, 1, 0)
    at = levels - (PAD - 8)
    set_faces(coef, masks[:, at, :], masks[:, at + 1, :], masks[:, at + 2, :], top)
    line = lax.broadcasted_iota(jnp.int32, (BAND, LANES), 1)
    for k in range(5):
        here, beyond = coef[k, :, :LANES], coef[k, :, LANES:]
        edge = jnp.where(line < half_turn, pltpu.roll(here, half_turn, 1), pltpu.roll(beyond, half_turn, 1))
        edge = jnp.where(line < half_turn - HALO, here, edge)
        strip_coef[k] = jnp.where(line >= LANES - HALO, beyond, edge)
    diffuse_all(strip, strip_next, strip_coef, 2, BAND - 2)
    physical = other
    for index in range(EDGE_ROW, EDGE_ROW + EDGE):
        edge = strip_next[index]
        turned = pltpu.roll(edge, half_turn, 1)
        physical[index, :, :LANES] = jnp.where(
            lane < 3, edge, jnp.where(lane >= LANES - 3, turned, inner_ref[index])
        )
        physical[index, :, LANES:] = jnp.where(lane < half_turn, turned, edge)

    for band in range(3):
        for half in range(2):
            cut = slice(half * LANES, (half + 1) * LANES)
            slot = 2 + 2 * band + half
            first, second = qa_ref[slot], qb_ref[slot]
            mid = (ns_ref[1, HALO + half], own_ref[ROWS + half], ns_ref[0, HALO + half])[band]
            obs[0, band, :, cut] = jnp.where(lon_even, second, first)
            obs[1, band, :, cut] = jnp.where(lon_even, first, second)
            obs[2, band, :, cut] = mid
    adj[...] = jnp.zeros(adj.shape, jnp.float32)
    cells = lax.broadcasted_iota(jnp.int32, (width, width), 0)
    keep = lax.broadcasted_iota(jnp.int32, (PAD, width), 0) < levels

    def places(side, band):
        base = obs[side, band, levels : levels + 1, :].astype(jnp.int32)
        p = obs[side, band, levels + 1 : levels + 2, :]
        q = obs[side, band, levels + 2 : levels + 3, :]
        j, i = base >> 7, base & (LANES - 1)
        turned = (top if band == NORTH else 0 * top) == 1
        rows = jnp.where(turned, 22 - j, j + ROWS * band)
        cols = jnp.where(turned, 126 - i, i)
        a0, a1 = jnp.where(turned, p, 1.0 - p), jnp.where(turned, 1.0 - p, p)
        b0, b1 = jnp.where(turned, q, 1.0 - q), jnp.where(turned, 1.0 - q, q)
        return rows, cols, a0, a1, b0, b1

    def weigh(side, band, profile):
        return jnp.where(keep, obs[side, band] * profile, 0.0)

    place = lax.broadcasted_iota(jnp.int32, (PAD, width), 1)
    packed = jnp.zeros((PAD, width), jnp.float32)
    for k in range(EDGE):
        cell = physical[EDGE_ROW + k]
        west = pltpu.roll(cell, (EDGE * k + 4) % width, 1)
        east = pltpu.roll(cell, (EDGE * k + 140) % width, 1)
        packed = jnp.where(
            (place >= EDGE * k) & (place < EDGE * k + 8),
            west,
            jnp.where((place >= EDGE * k + 8) & (place < EDGE * k + EDGE), east, packed),
        )
    packed = split(packed)
    edge_row, edge_col = cells >> 4, cells & (EDGE - 1)

    def beside(step, total):
        side, band = step & 1, step >> 1
        rows, cols, a0, a1, b0, b1 = places(side, band)
        rows = rows - EDGE_ROW
        cols = cols + jnp.where(side == 0, -124, 12)
        row_weight = jnp.where(edge_row == rows, a0, jnp.where(edge_row == rows + 1, a1, 0.0))
        col_weight = jnp.where(edge_col == cols, b0, jnp.where(edge_col == cols + 1, b1, 0.0))
        rhs = split(row_weight * col_weight)
        weighted = weigh(side, band, dot3(packed, rhs, ((1,), (0,))))
        return total + dot3(split(weighted), rhs, ((1,), (1,)))

    total = jnp.zeros((PAD, width), jnp.float32)
    for step in range(6):
        total = beside(step, total)
    for k in range(1, EDGE - 1):
        west = pltpu.roll(total, (width - EDGE * k - 4) % width, 1)
        east = pltpu.roll(total, (2 * width - EDGE * k - 140) % width, 1)
        adj[EDGE_ROW + k] = jnp.where(
            (place < 4) | (place >= width - 4),
            west,
            jnp.where((place >= 124) & (place < 132), east, 0.0),
        )

    for band, (begin, stop, lo, hi) in enumerate(((4, 9, 5, 9), (8, 17, 8, 17), (16, 20, 16, 19))):
        lhs = split(physical[begin:stop].reshape((stop - begin) * PAD, width))
        rows, cols, a0, a1, b0, b1 = places(2, band)
        lane0 = cols & (width - 1)
        lane1 = (cols + 1) & (width - 1)
        rhs = split(jnp.where(cells == lane0, b0, jnp.where(cells == lane1, b1, 0.0)))
        taken = dot3(lhs, rhs, ((1,), (0,)))
        row_weight = [
            jnp.where(rows == r, a0, jnp.where(rows == r - 1, a1, 0.0)) for r in range(begin, stop)
        ]
        profile = jnp.zeros((PAD, width), jnp.float32)
        for k in range(stop - begin):
            profile = profile + row_weight[k] * taken[k * PAD : (k + 1) * PAD]
        weighted = weigh(2, band, profile)
        spread = jnp.concatenate([row_weight[r - begin] * weighted for r in range(lo, hi)], 0)
        added = dot3(split(spread), rhs, ((1,), (1,)))
        adj[lo:hi] += added.reshape(hi - lo, PAD, width)

    diffuse_all(adj, other, coef, 6, BAND - 6)

    eof = split(eof_ref[...])
    rr = dim = rim = imim = jnp.zeros((levels, LANES), jnp.float32)
    for r in range(ROWS):
        back = dot3(eof, split(other[ROWS + r, :levels, :LANES]), ((0,), (0,)))
        d, res = dir_ref[:, r, :], res_ref[:, r, :]
        image = d + back
        img_ref[:, r, :] = image
        rr, dim, rim, imim = rr + res * res, dim + d * image, rim + res * image, imim + image * image
    lane = lax.broadcasted_iota(jnp.int32, part_ref.shape, 1)
    out = jnp.zeros(part_ref.shape, jnp.float32)
    for k, value in enumerate((rr, dim, rim, imim)):
        out = jnp.where(lane == k, jnp.sum(value), out)
    part_ref[...] = out


def finish(part_ref, img_ref, res_ref, dir_ref, new_res_ref, new_dir_ref, step_ref):
    total = jnp.sum(part_ref[...], axis=0, keepdims=True)
    lane = lax.broadcasted_iota(jnp.int32, total.shape, 1)
    rr, dim, rim, imim = (
        jnp.sum(jnp.where(lane == k, total, 0.0), axis=1, keepdims=True) for k in range(4)
    )
    step = rr / dim
    new_norm = rr + step * (step * imim - 2.0 * rim)
    beta = new_norm / rr
    step_ref[...] = step
    new_res = res_ref[...] - step[None] * img_ref[...]
    new_res_ref[...] = new_res
    new_dir_ref[...] = new_res + beta[None] * dir_ref[...]


def lat_pairs(lon_count, lat_count):
    index = lambda lon, lat: lon * lat_count + lat
    first, second = [], []
    for lon in range(lon_count):
        for lat in range(lat_count):
            first.append((index(lon, lat), index(lon, lat ^ 1)))
            other = lat + 1 if lat % 2 else lat - 1
            if other == lat_count:
                second.append((index(lon, lat), index(lon_count - 1 - lon, lat)))
            elif other >= 0:
                second.append((index(lon, lat), index(lon, other)))
    return first, second


def lon_pairs(lon_count):
    first = [(lon, lon ^ 1) for lon in range(lon_count)]
    second = [(lon, (lon + 1 if lon % 2 else lon - 1) % lon_count) for lon in range(lon_count)]
    return first, second


def per_device(
    direction, residual, eof_basis, kappa_east, kappa_north, wet_mask, obs_base, obs_frac, obs_rinv
):
    levels = direction.shape[0]
    shape = functools.partial(jax.ShapeDtypeStruct, dtype=jnp.float32)
    local = functools.partial(pltpu.VMEM, dtype=jnp.float32)
    lon_count, lat_count = lax.axis_size("lon"), lax.axis_size("lat")
    lon, lat = lax.axis_index("lon"), lax.axis_index("lat")
    flags = jnp.stack([1 - lat % 2, 1 - lon % 2, (lat == lat_count - 1).astype(jnp.int32)])
    flags = flags.astype(jnp.int32)
    inputs = (
        direction,
        eof_basis,
        kappa_east,
        kappa_north,
        wet_mask,
        obs_base.reshape(1, -1),
        obs_frac.reshape(2, 1, -1),
        obs_rinv.reshape(levels, 1, -1),
    )
    own, far, close = pl.pallas_call(
        pack_tile,
        out_shape=(
            local((ROWS + 2, PAD, LANES)),
            local((HALO + 2, PAD, LANES)),
            local((HALO + 2, PAD, LANES)),
        ),
        in_specs=[pl.BlockSpec(memory_space=pltpu.HBM)] * len(inputs),
        out_specs=(VMEM,) * 3,
        scratch_shapes=[pltpu.VMEM(x.shape, x.dtype) for x in inputs]
        + [pltpu.SemaphoreType.DMA((len(inputs),))],
        compiler_params=grant(8),
    )(*(pltpu.with_memory_space_constraint(x, pltpu.HBM) for x in inputs))
    direction, residual = near(direction), near(residual)
    first, second = lat_pairs(lon_count, lat_count)
    lat_b = lax.ppermute(far, ("lon", "lat"), second)
    lat_a = lax.ppermute(close, ("lon", "lat"), first)
    own, lat_a, lat_b = near(own), near(lat_a), near(lat_b)
    north_south, to_a, to_b = pl.pallas_call(
        pack_columns,
        out_shape=(local((2, HALO + 2, PAD, LANES)), local((8, PAD, LANES)), local((8, PAD, LANES))),
        in_specs=[SMEM] + [VMEM] * 3,
        out_specs=(VMEM,) * 3,
        compiler_params=grant(8),
    )(flags, own, lat_a, lat_b)
    first, second = lon_pairs(lon_count)
    tile = pltpu.VMEM((BAND, PAD, LANES), jnp.float32)
    wide = pltpu.VMEM((BAND, PAD, 2 * LANES), jnp.float32)
    inner = pl.pallas_call(
        functools.partial(inner_tile, levels),
        out_shape=local((BAND, PAD, LANES)),
        in_specs=[SMEM] + [VMEM] * 2,
        out_specs=VMEM,
        scratch_shapes=[tile, pltpu.VMEM((5, BAND, LANES), jnp.float32)],
        compiler_params=grant(8),
        cost_estimate=pl.CostEstimate(
            flops=10_000_000, bytes_accessed=2_000_000, transcendentals=0
        ),
    )(flags, own, near(north_south))
    lon_b = lax.ppermute(to_b, "lon", second)
    lon_a = lax.ppermute(to_a, "lon", first)
    image, part = pl.pallas_call(
        local_image,
        out_shape=(local(direction.shape), local((lon_count, LANES))),
        in_specs=[SMEM] + [VMEM] * 8,
        out_specs=(VMEM,) * 2,
        compiler_params=grant(28),
        scratch_shapes=[
            tile,
            tile,
            pltpu.VMEM((BAND, 8, 2 * LANES), jnp.float32),
            wide,
            wide,
            pltpu.VMEM((5, BAND, 2 * LANES), jnp.float32),
            pltpu.VMEM((5, BAND, LANES), jnp.float32),
            pltpu.VMEM((3, 3, PAD, 2 * LANES), jnp.float32),
        ],
    )(
        flags,
        own,
        near(north_south),
        near(lon_a),
        near(lon_b),
        direction,
        residual,
        near(eof_basis),
        near(inner),
    )
    part = lax.all_to_all(part, "lon", 0, 0, tiled=True)
    part = jnp.broadcast_to(jnp.sum(part, axis=0, keepdims=True), (lat_count, LANES))
    part = lax.all_to_all(part, "lat", 0, 0, tiled=True)
    new_residual, new_direction, step_length = pl.pallas_call(
        finish,
        out_shape=(shape(direction.shape), shape(direction.shape), shape((1, 1))),
        in_specs=[VMEM] * 4,
        out_specs=(VMEM,) * 3,
        compiler_params=grant(8),
    )(near(part), near(image), residual, direction)
    return new_residual, new_direction, step_length.reshape(())


def solution(mesh):
    return jax.shard_map(
        per_device,
        mesh=mesh,
        in_specs=(
            P(None, "lat", "lon"),
            P(None, "lat", "lon"),
            P(),
            P("lat", "lon"),
            P("lat", "lon"),
            P("lat", "lon"),
            P("lat", "lon", None),
            P(None, "lat", "lon", None),
            P(None, "lat", "lon", None),
        ),
        out_specs=(P(None, "lat", "lon"), P(None, "lat", "lon"), P()),
        check_vma=False,
    )
```

```python
import functools

import jax
import jax.numpy as jnp
from jax import lax
from jax.experimental import pallas as pl
from jax.experimental.pallas import tpu as pltpu
from jax.sharding import PartitionSpec as P


HIGHEST = lax.Precision.HIGHEST
LANES = 128
ROWS = 8
PAD = 80
BAND = 3 * ROWS
HALO = 7
SLOTS = 12
SOUTH, OWN, NORTH = 0, 1, 2
EDGE, EDGE_ROW = 16, 4

SMEM = pl.BlockSpec(memory_space=pltpu.SMEM)
VMEM = pl.BlockSpec(memory_space=pltpu.VMEM)


def grant(mebibytes):
    return pltpu.CompilerParams(vmem_limit_bytes=mebibytes << 20)


def near(x):
    return pltpu.with_memory_space_constraint(x, pltpu.VMEM)


def split(x):
    high = x.astype(jnp.bfloat16)
    return high, (x - high.astype(jnp.float32)).astype(jnp.bfloat16)


def dot3(left, right, dims):
    (lh, ll), (rh, rl) = left, right
    mul = functools.partial(
        lax.dot_general, dimension_numbers=(dims, ((), ())), preferred_element_type=jnp.float32
    )
    return mul(lh, rh) + (mul(lh, rl) + mul(ll, rh))


def pack_tile(*refs):
    count = (len(refs) - 4) // 2
    sources, held, sems = refs[:count], refs[count + 3 : -1], refs[-1]
    out_ref, far_ref, near_ref = refs[count : count + 3]
    copies = [
        pltpu.make_async_copy(source, target, sems.at[k])
        for k, (source, target) in enumerate(zip(sources, held))
    ]
    for copy in copies:
        copy.start()
    for copy in copies:
        copy.wait()
    dir_ref, eof_ref, ke_ref, kn_ref, wet_ref, base_ref, frac_ref, rinv_ref = held
    levels = dir_ref.shape[0]
    zeros = jnp.zeros((PAD - levels - 3, LANES), jnp.float32)
    eof = eof_ref[...]
    for row in range(ROWS):
        out_ref[row, :levels, :] = jnp.dot(
            eof, dir_ref[:, row, :], precision=HIGHEST, preferred_element_type=jnp.float32
        )
        out_ref[row, levels : levels + 1, :] = ke_ref[row : row + 1, :]
        out_ref[row, levels + 1 : levels + 2, :] = kn_ref[row : row + 1, :]
        out_ref[row, levels + 2 : levels + 3, :] = wet_ref[row : row + 1, :].astype(jnp.float32)
        out_ref[row, levels + 3 :, :] = zeros
    for half in range(2):
        cut = slice(half * LANES, (half + 1) * LANES)
        for level in range(levels):
            out_ref[ROWS + half, level : level + 1, :] = rinv_ref[level, :, cut]
        out_ref[ROWS + half, levels : levels + 1, :] = base_ref[:, cut].astype(jnp.float32)
        out_ref[ROWS + half, levels + 1 : levels + 2, :] = frac_ref[0, :, cut]
        out_ref[ROWS + half, levels + 2 : levels + 3, :] = frac_ref[1, :, cut]
        out_ref[ROWS + half, levels + 3 :, :] = zeros
        far_ref[HALO + half] = out_ref[ROWS + half]
        near_ref[HALO + half] = out_ref[ROWS + half]
    northern = lax.axis_index("lat") % 2 == 1
    for row in range(HALO):
        low, high = out_ref[row], out_ref[row + 1]
        far_ref[row] = jnp.where(northern, high, low)
        near_ref[row] = jnp.where(northern, low, high)


def row_tile(own_ref, ns_ref, index):
    if index in (0, BAND - 1):
        return None
    if index < ROWS:
        return ns_ref[1, index - 1]
    return own_ref[index - ROWS] if index < 2 * ROWS else ns_ref[0, index - 2 * ROWS]


def pack_columns(flags, own_ref, ra_ref, rb_ref, ns_ref, pa_ref, pb_ref):
    lat_even, lon_even, is_top = flags[0] == 1, flags[1] == 1, flags[2] == 1

    @pl.when(lat_even)
    def _():
        ns_ref[0] = ra_ref[...]
        ns_ref[1] = rb_ref[...]

    @pl.when(jnp.logical_not(lat_even))
    def _():
        ns_ref[0] = rb_ref[...]
        ns_ref[1] = ra_ref[...]

    @pl.when(is_top)
    def _():
        first = lax.broadcasted_iota(jnp.int32, (LANES, LANES), 0)
        second = lax.broadcasted_iota(jnp.int32, (LANES, LANES), 1)
        flip = jnp.where(first + second == LANES - 1, 1.0, 0.0).astype(jnp.float32)
        for row in range(HALO):
            ns_ref[0, row] = jnp.dot(
                rb_ref[HALO - 1 - row], flip, precision=HIGHEST, preferred_element_type=jnp.float32
            )

    lane = lax.broadcasted_iota(jnp.int32, (PAD, LANES), 1)
    for group in range(2):
        west = jnp.zeros((PAD, LANES), jnp.float32)
        east = jnp.zeros((PAD, LANES), jnp.float32)
        for slot in range(SLOTS):
            tile = row_tile(own_ref, ns_ref, group * SLOTS + slot)
            if tile is None:
                continue
            start = HALO * slot
            here = (lane >= start) & (lane < start + HALO)
            west = jnp.where(here, pltpu.roll(tile, start, 1) if start else tile, west)
            east = jnp.where(here, pltpu.roll(tile, (start + HALO) % LANES, 1), east)
        pa_ref[group] = jnp.where(lon_even, east, west)
        pb_ref[group] = jnp.where(lon_even, west, east)
    for half in range(2):
        for ref in (pa_ref, pb_ref):
            ref[2 + 2 * SOUTH + half] = ns_ref[1, HALO + half]
            ref[2 + 2 * OWN + half] = own_ref[ROWS + half]
            ref[2 + 2 * NORTH + half] = ns_ref[0, HALO + half]


def diffuse_row(src, dst, coef, index):
    centre = src[index]
    width = centre.shape[1]
    wide = lambda k: jnp.broadcast_to(coef[k, pl.ds(index, 1), :], centre.shape)
    out = centre * wide(0)
    out = out + wide(1) * pltpu.roll(centre, width - 1, 1)
    out = out + wide(2) * pltpu.roll(centre, 1, 1)
    out = out + wide(3) * src[index + 1]
    out = out + wide(4) * src[index - 1]
    dst[index] = out


def diffuse_own(src, dst, coef, index):
    own, beyond = src[index, :, :LANES], src[index, :, LANES:]
    lane = lax.broadcasted_iota(jnp.int32, own.shape, 1)
    wide = lambda k: jnp.broadcast_to(coef[k, pl.ds(index, 1), :LANES], own.shape)
    out = own * wide(0)
    out = out + wide(1) * pltpu.roll(jnp.where(lane == 0, beyond, own), LANES - 1, 1)
    out = out + wide(2) * pltpu.roll(jnp.where(lane == LANES - 1, beyond, own), 1, 1)
    out = out + wide(3) * src[index + 1, :, :LANES]
    out = out + wide(4) * src[index - 1, :, :LANES]
    dst[index, :, :LANES] = out


def diffuse_all(one, two, coef, low, high, last=diffuse_row):
    for src, dst, trim, step in (
        (one, two, 0, diffuse_row),
        (two, one, 1, diffuse_row),
        (one, two, 2, last),
    ):
        for index in range(low + trim, high - trim):
            step(src, dst, coef, index)


def local_image(
    flags,
    own_ref,
    ns_ref,
    qa_ref,
    qb_ref,
    dir_ref,
    res_ref,
    eoft_ref,
    img_ref,
    part_ref,
    field,
    other,
    adj,
    coef,
    obs,
):
    lon_even, is_top = flags[1] == 1, flags[2] == 1
    levels = dir_ref.shape[0]
    width = 2 * LANES
    lane = lax.broadcasted_iota(jnp.int32, (PAD, LANES), 1)
    for group in range(2):
        first, second = qa_ref[group], qb_ref[group]
        east = jnp.where(lon_even, first, second)
        west = jnp.where(lon_even, second, first)
        for slot in range(SLOTS):
            index = group * SLOTS + slot
            tile = row_tile(own_ref, ns_ref, index)
            if tile is None:
                field[index] = jnp.zeros((PAD, width), jnp.float32)
                continue
            start = HALO * slot
            from_east = pltpu.roll(east, (LANES - start) % LANES, 1) if start else east
            from_west = pltpu.roll(west, (LANES - HALO - start) % LANES, 1)
            field[index, :, :LANES] = tile
            field[index, :, LANES:] = jnp.where(
                lane < HALO, from_east, jnp.where(lane >= LANES - HALO, from_west, 0.0)
            )

    ke, kn, wet = field[:, levels, :], field[:, levels + 1, :], field[:, levels + 2, :]
    row = lax.broadcasted_iota(jnp.int32, (BAND, width), 0)
    up = lambda x: jnp.concatenate([x[1:], x[:1]], 0)
    down = lambda x: jnp.concatenate([x[-1:], x[:-1]], 0)
    right = lambda x: pltpu.roll(x, width - 1, 1)
    left = lambda x: pltpu.roll(x, 1, 1)
    seam = 2 * ROWS - 1
    top = jnp.where(is_top, 1, 0)
    ke = jnp.where((row > seam) & (top == 1), right(ke), ke)
    kn_up = up(kn)
    kn = jnp.where(
        top == 1, jnp.where(row > seam, kn_up, jnp.where(row == seam, 0.5 * (kn + kn_up), kn)), kn
    )
    east_face = ke * wet * right(wet)
    north_face = kn * wet * up(wet)
    west_face, south_face = left(east_face), down(north_face)
    coef[0] = 1.0 - east_face - west_face - north_face - south_face
    coef[1] = east_face
    coef[2] = west_face
    coef[3] = north_face
    coef[4] = south_face

    diffuse_all(field, other, coef, 2, BAND - 2)
    physical = other

    for band in range(3):
        for half in range(2):
            cut = slice(half * LANES, (half + 1) * LANES)
            slot = 2 + 2 * band + half
            first, second = qa_ref[slot], qb_ref[slot]
            mid = (ns_ref[1, HALO + half], own_ref[ROWS + half], ns_ref[0, HALO + half])[band]
            obs[0, band, :, cut] = jnp.where(lon_even, second, first)
            obs[1, band, :, cut] = jnp.where(lon_even, first, second)
            obs[2, band, :, cut] = mid
    adj[...] = jnp.zeros(adj.shape, jnp.float32)
    cells = lax.broadcasted_iota(jnp.int32, (width, width), 0)
    keep = lax.broadcasted_iota(jnp.int32, (PAD, width), 0) < levels

    def places(side, band):
        base = obs[side, band, levels : levels + 1, :].astype(jnp.int32)
        p = obs[side, band, levels + 1 : levels + 2, :]
        q = obs[side, band, levels + 2 : levels + 3, :]
        j, i = base >> 7, base & (LANES - 1)
        turned = (top if band == NORTH else 0 * top) == 1
        rows = jnp.where(turned, 22 - j, j + ROWS * band)
        cols = jnp.where(turned, 126 - i, i)
        a0, a1 = jnp.where(turned, p, 1.0 - p), jnp.where(turned, 1.0 - p, p)
        b0, b1 = jnp.where(turned, q, 1.0 - q), jnp.where(turned, 1.0 - q, q)
        return rows, cols, a0, a1, b0, b1

    def weigh(side, band, profile):
        return jnp.where(keep, obs[side, band] * profile, 0.0)

    packed = [jnp.zeros((PAD, LANES), jnp.float32)] * 2
    for k in range(EDGE):
        own, beyond = physical[EDGE_ROW + k, :, :LANES], physical[EDGE_ROW + k, :, LANES:]
        west = pltpu.roll(jnp.where(lane < LANES // 2, own, beyond), (EDGE * k + 4) % LANES, 1)
        east = pltpu.roll(jnp.where(lane < LANES // 2, beyond, own), (EDGE * k + 12) % LANES, 1)
        half, first = k // 8, EDGE * (k % 8)
        packed[half] = jnp.where(
            (lane >= first) & (lane < first + 8),
            west,
            jnp.where((lane >= first + 8) & (lane < first + EDGE), east, packed[half]),
        )
    packed = jnp.concatenate(packed, 1)
    packed = split(packed)
    edge_row, edge_col = cells >> 4, cells & (EDGE - 1)

    def beside(step, total):
        side, band = step & 1, step >> 1
        rows, cols, a0, a1, b0, b1 = places(side, band)
        rows = rows - EDGE_ROW
        cols = cols + jnp.where(side == 0, -124, 12)
        row_weight = jnp.where(edge_row == rows, a0, jnp.where(edge_row == rows + 1, a1, 0.0))
        col_weight = jnp.where(edge_col == cols, b0, jnp.where(edge_col == cols + 1, b1, 0.0))
        rhs = split(row_weight * col_weight)
        weighted = weigh(side, band, dot3(packed, rhs, ((1,), (0,))))
        return total + dot3(split(weighted), rhs, ((1,), (1,)))

    total = jnp.zeros((PAD, width), jnp.float32)
    for step in range(6):
        total = beside(step, total)
    for k in range(1, EDGE - 1):
        half = k // 8
        here = total[:, half * LANES : (half + 1) * LANES]
        west = pltpu.roll(here, (2 * LANES - EDGE * (k % 8) - 4) % LANES, 1)
        east = pltpu.roll(here, (2 * LANES - EDGE * (k % 8) - 12) % LANES, 1)
        low, high = lane < 4, lane >= LANES - 4
        adj[EDGE_ROW + k, :, :LANES] = jnp.where(low, west, jnp.where(high, east, 0.0))
        adj[EDGE_ROW + k, :, LANES:] = jnp.where(low, east, jnp.where(high, west, 0.0))

    for band, (begin, stop, lo, hi) in enumerate(((4, 9, 5, 9), (8, 17, 8, 17), (16, 20, 16, 19))):
        lhs = split(physical[begin:stop].reshape((stop - begin) * PAD, width))
        rows, cols, a0, a1, b0, b1 = places(2, band)
        lane0 = cols & (width - 1)
        lane1 = (cols + 1) & (width - 1)
        rhs = split(jnp.where(cells == lane0, b0, jnp.where(cells == lane1, b1, 0.0)))
        taken = dot3(lhs, rhs, ((1,), (0,)))
        row_weight = [
            jnp.where(rows == r, a0, jnp.where(rows == r - 1, a1, 0.0)) for r in range(begin, stop)
        ]
        profile = jnp.zeros((PAD, width), jnp.float32)
        for k in range(stop - begin):
            profile = profile + row_weight[k] * taken[k * PAD : (k + 1) * PAD]
        weighted = weigh(2, band, profile)
        spread = jnp.concatenate([row_weight[r - begin] * weighted for r in range(lo, hi)], 0)
        added = dot3(split(spread), rhs, ((1,), (1,)))
        adj[lo:hi] += added.reshape(hi - lo, PAD, width)

    diffuse_all(adj, other, coef, 6, BAND - 6, diffuse_own)

    eoft = split(eoft_ref[...])
    rr = dim = rim = imim = jnp.zeros((levels, LANES), jnp.float32)
    for r in range(ROWS):
        back = dot3(eoft, split(other[ROWS + r, :levels, :LANES]), ((1,), (0,)))
        d, res = dir_ref[:, r, :], res_ref[:, r, :]
        image = d + back
        img_ref[:, r, :] = image
        rr, dim, rim, imim = rr + res * res, dim + d * image, rim + res * image, imim + image * image
    lane = lax.broadcasted_iota(jnp.int32, part_ref.shape, 1)
    out = jnp.zeros(part_ref.shape, jnp.float32)
    for k, value in enumerate((rr, dim, rim, imim)):
        out = jnp.where(lane == k, jnp.sum(value), out)
    part_ref[...] = out


def finish(part_ref, img_ref, res_ref, dir_ref, new_res_ref, new_dir_ref, step_ref):
    total = jnp.sum(part_ref[...], axis=0, keepdims=True)
    lane = lax.broadcasted_iota(jnp.int32, total.shape, 1)
    rr, dim, rim, imim = (
        jnp.sum(jnp.where(lane == k, total, 0.0), axis=1, keepdims=True) for k in range(4)
    )
    step = rr / dim
    new_norm = rr + step * (step * imim - 2.0 * rim)
    beta = new_norm / rr
    step_ref[...] = step
    new_res = res_ref[...] - step[None] * img_ref[...]
    new_res_ref[...] = new_res
    new_dir_ref[...] = new_res + beta[None] * dir_ref[...]


def lat_pairs(lon_count, lat_count):
    index = lambda lon, lat: lon * lat_count + lat
    first, second = [], []
    for lon in range(lon_count):
        for lat in range(lat_count):
            first.append((index(lon, lat), index(lon, lat ^ 1)))
            other = lat + 1 if lat % 2 else lat - 1
            if other == lat_count:
                second.append((index(lon, lat), index(lon_count - 1 - lon, lat)))
            elif other >= 0:
                second.append((index(lon, lat), index(lon, other)))
    return first, second


def lon_pairs(lon_count):
    first = [(lon, lon ^ 1) for lon in range(lon_count)]
    second = [(lon, (lon + 1 if lon % 2 else lon - 1) % lon_count) for lon in range(lon_count)]
    return first, second


def per_device(
    direction, residual, eof_basis, kappa_east, kappa_north, wet_mask, obs_base, obs_frac, obs_rinv
):
    levels = direction.shape[0]
    shape = functools.partial(jax.ShapeDtypeStruct, dtype=jnp.float32)
    local = functools.partial(pltpu.VMEM, dtype=jnp.float32)
    lon_count, lat_count = lax.axis_size("lon"), lax.axis_size("lat")
    lon, lat = lax.axis_index("lon"), lax.axis_index("lat")
    flags = jnp.stack([1 - lat % 2, 1 - lon % 2, (lat == lat_count - 1).astype(jnp.int32)])
    flags = flags.astype(jnp.int32)
    inputs = (
        direction,
        eof_basis,
        kappa_east,
        kappa_north,
        wet_mask,
        obs_base.reshape(1, -1),
        obs_frac.reshape(2, 1, -1),
        obs_rinv.reshape(levels, 1, -1),
    )
    own, far, close = pl.pallas_call(
        pack_tile,
        out_shape=(
            local((ROWS + 2, PAD, LANES)),
            local((HALO + 2, PAD, LANES)),
            local((HALO + 2, PAD, LANES)),
        ),
        in_specs=[pl.BlockSpec(memory_space=pltpu.HBM)] * len(inputs),
        out_specs=(VMEM,) * 3,
        scratch_shapes=[pltpu.VMEM(x.shape, x.dtype) for x in inputs]
        + [pltpu.SemaphoreType.DMA((len(inputs),))],
        compiler_params=grant(8),
    )(*(pltpu.with_memory_space_constraint(x, pltpu.HBM) for x in inputs))
    direction, residual = near(direction), near(residual)
    first, second = lat_pairs(lon_count, lat_count)
    lat_b = lax.ppermute(far, ("lon", "lat"), second)
    lat_a = lax.ppermute(close, ("lon", "lat"), first)
    own, lat_a, lat_b = near(own), near(lat_a), near(lat_b)
    north_south, to_a, to_b = pl.pallas_call(
        pack_columns,
        out_shape=(local((2, HALO + 2, PAD, LANES)), local((8, PAD, LANES)), local((8, PAD, LANES))),
        in_specs=[SMEM] + [VMEM] * 3,
        out_specs=(VMEM,) * 3,
        compiler_params=grant(8),
    )(flags, own, lat_a, lat_b)
    first, second = lon_pairs(lon_count)
    lon_b = lax.ppermute(to_b, "lon", second)
    lon_a = lax.ppermute(to_a, "lon", first)
    image, part = pl.pallas_call(
        local_image,
        out_shape=(local(direction.shape), local((lon_count, LANES))),
        in_specs=[SMEM] + [VMEM] * 7,
        out_specs=(VMEM,) * 2,
        compiler_params=grant(28),
        scratch_shapes=[
            pltpu.VMEM((BAND, PAD, 2 * LANES), jnp.float32),
            pltpu.VMEM((BAND, PAD, 2 * LANES), jnp.float32),
            pltpu.VMEM((BAND, PAD, 2 * LANES), jnp.float32),
            pltpu.VMEM((5, BAND, 2 * LANES), jnp.float32),
            pltpu.VMEM((3, 3, PAD, 2 * LANES), jnp.float32),
        ],
    )(flags, own, near(north_south), near(lon_a), near(lon_b), direction, residual, near(eof_basis.T))
    part = lax.all_to_all(part, "lon", 0, 0, tiled=True)
    part = jnp.broadcast_to(jnp.sum(part, axis=0, keepdims=True), (lat_count, LANES))
    part = lax.all_to_all(part, "lat", 0, 0, tiled=True)
    new_residual, new_direction, step_length = pl.pallas_call(
        finish,
        out_shape=(shape(direction.shape), shape(direction.shape), shape((1, 1))),
        in_specs=[VMEM] * 4,
        out_specs=(VMEM,) * 3,
        compiler_params=grant(8),
    )(near(part), near(image), residual, direction)
    return new_residual, new_direction, step_length.reshape(())


def solution(mesh):
    return jax.shard_map(
        per_device,
        mesh=mesh,
        in_specs=(
            P(None, "lat", "lon"),
            P(None, "lat", "lon"),
            P(),
            P("lat", "lon"),
            P("lat", "lon"),
            P("lat", "lon"),
            P("lat", "lon", None),
            P(None, "lat", "lon", None),
            P(None, "lat", "lon", None),
        ),
        out_specs=(P(None, "lat", "lon"), P(None, "lat", "lon"), P()),
        check_vma=False,
    )
```

```python
import functools

import jax
import jax.numpy as jnp
from jax import lax
from jax.experimental import pallas as pl
from jax.experimental.pallas import tpu as pltpu
from jax.sharding import PartitionSpec as P


HIGHEST = lax.Precision.HIGHEST
LANES = 128
ROWS = 8
PAD = 80
BAND = 3 * ROWS
HALO = 7
SLOTS = 12
SOUTH, OWN, NORTH = 0, 1, 2
EDGE, EDGE_ROW = 16, 4

SMEM = pl.BlockSpec(memory_space=pltpu.SMEM)
VMEM = pl.BlockSpec(memory_space=pltpu.VMEM)


def grant(mebibytes):
    return pltpu.CompilerParams(vmem_limit_bytes=mebibytes << 20)


def near(x):
    return pltpu.with_memory_space_constraint(x, pltpu.VMEM)


def split(x):
    high = x.astype(jnp.bfloat16)
    return high, (x - high.astype(jnp.float32)).astype(jnp.bfloat16)


def dot3(left, right, dims):
    (lh, ll), (rh, rl) = left, right
    mul = functools.partial(
        lax.dot_general, dimension_numbers=(dims, ((), ())), preferred_element_type=jnp.float32
    )
    return mul(lh, rh) + (mul(lh, rl) + mul(ll, rh))


def pack_tile(*refs):
    count = (len(refs) - 4) // 2
    sources, held, sems = refs[:count], refs[count + 3 : -1], refs[-1]
    out_ref, far_ref, near_ref = refs[count : count + 3]
    copies = [
        pltpu.make_async_copy(source, target, sems.at[k])
        for k, (source, target) in enumerate(zip(sources, held))
    ]
    for copy in copies:
        copy.start()
    for copy in copies:
        copy.wait()
    dir_ref, eof_ref, ke_ref, kn_ref, wet_ref, base_ref, frac_ref, rinv_ref = held
    levels = dir_ref.shape[0]
    zeros = jnp.zeros((PAD - levels - 3, LANES), jnp.float32)
    eof = eof_ref[...]
    for row in range(ROWS):
        out_ref[row, :levels, :] = jnp.dot(
            eof, dir_ref[:, row, :], precision=HIGHEST, preferred_element_type=jnp.float32
        )
        out_ref[row, levels : levels + 1, :] = ke_ref[row : row + 1, :]
        out_ref[row, levels + 1 : levels + 2, :] = kn_ref[row : row + 1, :]
        out_ref[row, levels + 2 : levels + 3, :] = wet_ref[row : row + 1, :].astype(jnp.float32)
        out_ref[row, levels + 3 :, :] = zeros
    for half in range(2):
        cut = slice(half * LANES, (half + 1) * LANES)
        for level in range(levels):
            out_ref[ROWS + half, level : level + 1, :] = rinv_ref[level, :, cut]
        out_ref[ROWS + half, levels : levels + 1, :] = base_ref[:, cut].astype(jnp.float32)
        out_ref[ROWS + half, levels + 1 : levels + 2, :] = frac_ref[0, :, cut]
        out_ref[ROWS + half, levels + 2 : levels + 3, :] = frac_ref[1, :, cut]
        out_ref[ROWS + half, levels + 3 :, :] = zeros
        far_ref[HALO + half] = out_ref[ROWS + half]
        near_ref[HALO + half] = out_ref[ROWS + half]
    northern = lax.axis_index("lat") % 2 == 1
    for row in range(HALO):
        low, high = out_ref[row], out_ref[row + 1]
        far_ref[row] = jnp.where(northern, high, low)
        near_ref[row] = jnp.where(northern, low, high)


def by_rows(dir_ref, res_ref, dir_rows_ref, res_rows_ref):
    for source, target in ((dir_ref, dir_rows_ref), (res_ref, res_rows_ref)):
        for row in range(ROWS):
            target[row, : source.shape[0], :] = source[:, row, :]


def row_tile(own_ref, ns_ref, index):
    if index in (0, BAND - 1):
        return None
    if index < ROWS:
        return ns_ref[1, index - 1]
    return own_ref[index - ROWS] if index < 2 * ROWS else ns_ref[0, index - 2 * ROWS]


def pack_columns(flags, own_ref, ra_ref, rb_ref, ns_ref, pa_ref, pb_ref):
    lat_even, lon_even, is_top = flags[0] == 1, flags[1] == 1, flags[2] == 1

    @pl.when(lat_even)
    def _():
        ns_ref[0] = ra_ref[...]
        ns_ref[1] = rb_ref[...]

    @pl.when(jnp.logical_not(lat_even))
    def _():
        ns_ref[0] = rb_ref[...]
        ns_ref[1] = ra_ref[...]

    @pl.when(is_top)
    def _():
        first = lax.broadcasted_iota(jnp.int32, (LANES, LANES), 0)
        second = lax.broadcasted_iota(jnp.int32, (LANES, LANES), 1)
        flip = jnp.where(first + second == LANES - 1, 1.0, 0.0).astype(jnp.float32)
        for row in range(HALO):
            ns_ref[0, row] = jnp.dot(
                rb_ref[HALO - 1 - row], flip, precision=HIGHEST, preferred_element_type=jnp.float32
            )

    lane = lax.broadcasted_iota(jnp.int32, (PAD, LANES), 1)
    for group in range(2):
        west = jnp.zeros((PAD, LANES), jnp.float32)
        east = jnp.zeros((PAD, LANES), jnp.float32)
        for slot in range(SLOTS):
            tile = row_tile(own_ref, ns_ref, group * SLOTS + slot)
            if tile is None:
                continue
            start = HALO * slot
            here = (lane >= start) & (lane < start + HALO)
            west = jnp.where(here, pltpu.roll(tile, start, 1) if start else tile, west)
            east = jnp.where(here, pltpu.roll(tile, (start + HALO) % LANES, 1), east)
        pa_ref[group] = jnp.where(lon_even, east, west)
        pb_ref[group] = jnp.where(lon_even, west, east)
    for half in range(2):
        for ref in (pa_ref, pb_ref):
            ref[2 + 2 * SOUTH + half] = ns_ref[1, HALO + half]
            ref[2 + 2 * OWN + half] = own_ref[ROWS + half]
            ref[2 + 2 * NORTH + half] = ns_ref[0, HALO + half]


def diffuse_row(src, dst, coef, index):
    centre = src[index]
    width = centre.shape[1]
    wide = lambda k: jnp.broadcast_to(coef[k, pl.ds(index, 1), :], centre.shape)
    out = centre * wide(0)
    out = out + wide(1) * pltpu.roll(centre, width - 1, 1)
    out = out + wide(2) * pltpu.roll(centre, 1, 1)
    out = out + wide(3) * src[index + 1]
    out = out + wide(4) * src[index - 1]
    dst[index] = out


def diffuse_own(src, dst, coef, index):
    own, beyond = src[index, :, :LANES], src[index, :, LANES:]
    lane = lax.broadcasted_iota(jnp.int32, own.shape, 1)
    wide = lambda k: jnp.broadcast_to(coef[k, pl.ds(index, 1), :LANES], own.shape)
    out = own * wide(0)
    out = out + wide(1) * pltpu.roll(jnp.where(lane == 0, beyond, own), LANES - 1, 1)
    out = out + wide(2) * pltpu.roll(jnp.where(lane == LANES - 1, beyond, own), 1, 1)
    out = out + wide(3) * src[index + 1, :, :LANES]
    out = out + wide(4) * src[index - 1, :, :LANES]
    dst[index, :, :LANES] = out


def diffuse_all(one, two, coef, low, high, last=diffuse_row):
    for src, dst, trim, step in (
        (one, two, 0, diffuse_row),
        (two, one, 1, diffuse_row),
        (one, two, 2, last),
    ):
        for index in range(low + trim, high - trim):
            step(src, dst, coef, index)


def local_image(
    flags,
    own_ref,
    ns_ref,
    qa_ref,
    qb_ref,
    dir_ref,
    res_ref,
    eoft_ref,
    img_ref,
    part_ref,
    field,
    other,
    adj,
    coef,
    obs,
):
    lon_even, is_top = flags[1] == 1, flags[2] == 1
    levels = img_ref.shape[0]
    width = 2 * LANES
    lane = lax.broadcasted_iota(jnp.int32, (PAD, LANES), 1)
    for group in range(2):
        first, second = qa_ref[group], qb_ref[group]
        east = jnp.where(lon_even, first, second)
        west = jnp.where(lon_even, second, first)
        for slot in range(SLOTS):
            index = group * SLOTS + slot
            tile = row_tile(own_ref, ns_ref, index)
            if tile is None:
                field[index] = jnp.zeros((PAD, width), jnp.float32)
                continue
            start = HALO * slot
            from_east = pltpu.roll(east, (LANES - start) % LANES, 1) if start else east
            from_west = pltpu.roll(west, (LANES - HALO - start) % LANES, 1)
            field[index, :, :LANES] = tile
            field[index, :, LANES:] = jnp.where(
                lane < HALO, from_east, jnp.where(lane >= LANES - HALO, from_west, 0.0)
            )

    ke, kn, wet = field[:, levels, :], field[:, levels + 1, :], field[:, levels + 2, :]
    row = lax.broadcasted_iota(jnp.int32, (BAND, width), 0)
    up = lambda x: jnp.concatenate([x[1:], x[:1]], 0)
    down = lambda x: jnp.concatenate([x[-1:], x[:-1]], 0)
    right = lambda x: pltpu.roll(x, width - 1, 1)
    left = lambda x: pltpu.roll(x, 1, 1)
    seam = 2 * ROWS - 1
    top = jnp.where(is_top, 1, 0)
    ke = jnp.where((row > seam) & (top == 1), right(ke), ke)
    kn_up = up(kn)
    kn = jnp.where(
        top == 1, jnp.where(row > seam, kn_up, jnp.where(row == seam, 0.5 * (kn + kn_up), kn)), kn
    )
    east_face = ke * wet * right(wet)
    north_face = kn * wet * up(wet)
    west_face, south_face = left(east_face), down(north_face)
    coef[0] = 1.0 - east_face - west_face - north_face - south_face
    coef[1] = east_face
    coef[2] = west_face
    coef[3] = north_face
    coef[4] = south_face

    diffuse_all(field, other, coef, 2, BAND - 2)
    physical = other

    for band in range(3):
        for half in range(2):
            cut = slice(half * LANES, (half + 1) * LANES)
            slot = 2 + 2 * band + half
            first, second = qa_ref[slot], qb_ref[slot]
            mid = (ns_ref[1, HALO + half], own_ref[ROWS + half], ns_ref[0, HALO + half])[band]
            obs[0, band, :, cut] = jnp.where(lon_even, second, first)
            obs[1, band, :, cut] = jnp.where(lon_even, first, second)
            obs[2, band, :, cut] = mid
    adj[...] = jnp.zeros(adj.shape, jnp.float32)
    cells = lax.broadcasted_iota(jnp.int32, (width, width), 0)
    keep = lax.broadcasted_iota(jnp.int32, (PAD, width), 0) < levels

    def places(side, band):
        base = obs[side, band, levels : levels + 1, :].astype(jnp.int32)
        p = obs[side, band, levels + 1 : levels + 2, :]
        q = obs[side, band, levels + 2 : levels + 3, :]
        j, i = base >> 7, base & (LANES - 1)
        turned = (top if band == NORTH else 0 * top) == 1
        rows = jnp.where(turned, 22 - j, j + ROWS * band)
        cols = jnp.where(turned, 126 - i, i)
        a0, a1 = jnp.where(turned, p, 1.0 - p), jnp.where(turned, 1.0 - p, p)
        b0, b1 = jnp.where(turned, q, 1.0 - q), jnp.where(turned, 1.0 - q, q)
        return rows, cols, a0, a1, b0, b1

    def weigh(side, band, profile):
        return jnp.where(keep, obs[side, band] * profile, 0.0)

    packed = [jnp.zeros((PAD, LANES), jnp.float32)] * 2
    for k in range(EDGE):
        own, beyond = physical[EDGE_ROW + k, :, :LANES], physical[EDGE_ROW + k, :, LANES:]
        west = pltpu.roll(jnp.where(lane < LANES // 2, own, beyond), (EDGE * k + 4) % LANES, 1)
        east = pltpu.roll(jnp.where(lane < LANES // 2, beyond, own), (EDGE * k + 12) % LANES, 1)
        half, first = k // 8, EDGE * (k % 8)
        packed[half] = jnp.where(
            (lane >= first) & (lane < first + 8),
            west,
            jnp.where((lane >= first + 8) & (lane < first + EDGE), east, packed[half]),
        )
    packed = jnp.concatenate(packed, 1)
    packed = split(packed)
    edge_col = lax.broadcasted_iota(jnp.int32, (EDGE, width), 0)

    def beside(step, total):
        side, band = step & 1, step >> 1
        rows, cols, a0, a1, b0, b1 = places(side, band)
        rows = rows - EDGE_ROW
        cols = cols + jnp.where(side == 0, -124, 12)
        col_weight = jnp.where(edge_col == cols, b0, jnp.where(edge_col == cols + 1, b1, 0.0))
        rows, a0, a1 = (jnp.broadcast_to(x, (8, width)) for x in (rows, a0, a1))
        parts = []
        for k in range(EDGE):
            row_weight = jnp.where(rows == k, a0, jnp.where(rows == k - 1, a1, 0.0))
            parts += [row_weight * col_weight[:8], row_weight * col_weight[8:]]
        rhs = split(jnp.concatenate(parts, 0))
        weighted = weigh(side, band, dot3(packed, rhs, ((1,), (0,))))
        return total + dot3(split(weighted), rhs, ((1,), (1,)))

    total = jnp.zeros((PAD, width), jnp.float32)
    for step in range(6):
        total = beside(step, total)
    for k in range(1, EDGE - 1):
        half = k // 8
        here = total[:, half * LANES : (half + 1) * LANES]
        west = pltpu.roll(here, (2 * LANES - EDGE * (k % 8) - 4) % LANES, 1)
        east = pltpu.roll(here, (2 * LANES - EDGE * (k % 8) - 12) % LANES, 1)
        low, high = lane < 4, lane >= LANES - 4
        adj[EDGE_ROW + k, :, :LANES] = jnp.where(low, west, jnp.where(high, east, 0.0))
        adj[EDGE_ROW + k, :, LANES:] = jnp.where(low, east, jnp.where(high, west, 0.0))

    for band, (begin, stop, lo, hi) in enumerate(((4, 9, 5, 9), (8, 17, 8, 17), (16, 20, 16, 19))):
        lhs = split(physical[begin:stop].reshape((stop - begin) * PAD, width))
        rows, cols, a0, a1, b0, b1 = places(2, band)
        lane0 = cols & (width - 1)
        lane1 = (cols + 1) & (width - 1)
        rhs = split(jnp.where(cells == lane0, b0, jnp.where(cells == lane1, b1, 0.0)))
        taken = dot3(lhs, rhs, ((1,), (0,)))
        row_weight = [
            jnp.where(rows == r, a0, jnp.where(rows == r - 1, a1, 0.0)) for r in range(begin, stop)
        ]
        profile = jnp.zeros((PAD, width), jnp.float32)
        for k in range(stop - begin):
            profile = profile + row_weight[k] * taken[k * PAD : (k + 1) * PAD]
        weighted = weigh(2, band, profile)
        spread = jnp.concatenate([row_weight[r - begin] * weighted for r in range(lo, hi)], 0)
        added = dot3(split(spread), rhs, ((1,), (1,)))
        adj[lo:hi] += added.reshape(hi - lo, PAD, width)

    diffuse_all(adj, other, coef, 6, BAND - 6, diffuse_own)

    eoft = split(eoft_ref[...])
    rr = dim = rim = imim = jnp.zeros((levels, LANES), jnp.float32)
    for r in range(ROWS):
        back = dot3(eoft, split(other[ROWS + r, :levels, :LANES]), ((1,), (0,)))
        d, res = dir_ref[r, :levels, :], res_ref[r, :levels, :]
        image = d + back
        img_ref[:, r, :] = image
        rr, dim, rim, imim = rr + res * res, dim + d * image, rim + res * image, imim + image * image
    lane = lax.broadcasted_iota(jnp.int32, part_ref.shape, 1)
    out = jnp.zeros(part_ref.shape, jnp.float32)
    for k, value in enumerate((rr, dim, rim, imim)):
        out = jnp.where(lane == k, jnp.sum(value), out)
    part_ref[...] = out


def finish(part_ref, img_ref, res_ref, dir_ref, new_res_ref, new_dir_ref, step_ref):
    total = jnp.sum(part_ref[...], axis=0, keepdims=True)
    lane = lax.broadcasted_iota(jnp.int32, total.shape, 1)
    rr, dim, rim, imim = (
        jnp.sum(jnp.where(lane == k, total, 0.0), axis=1, keepdims=True) for k in range(4)
    )
    step = rr / dim
    new_norm = rr + step * (step * imim - 2.0 * rim)
    beta = new_norm / rr
    step_ref[...] = step
    new_res = res_ref[...] - step[None] * img_ref[...]
    new_res_ref[...] = new_res
    new_dir_ref[...] = new_res + beta[None] * dir_ref[...]


def lat_pairs(lon_count, lat_count):
    index = lambda lon, lat: lon * lat_count + lat
    first, second = [], []
    for lon in range(lon_count):
        for lat in range(lat_count):
            first.append((index(lon, lat), index(lon, lat ^ 1)))
            other = lat + 1 if lat % 2 else lat - 1
            if other == lat_count:
                second.append((index(lon, lat), index(lon_count - 1 - lon, lat)))
            elif other >= 0:
                second.append((index(lon, lat), index(lon, other)))
    return first, second


def lon_pairs(lon_count):
    first = [(lon, lon ^ 1) for lon in range(lon_count)]
    second = [(lon, (lon + 1 if lon % 2 else lon - 1) % lon_count) for lon in range(lon_count)]
    return first, second


def per_device(
    direction, residual, eof_basis, kappa_east, kappa_north, wet_mask, obs_base, obs_frac, obs_rinv
):
    levels = direction.shape[0]
    shape = functools.partial(jax.ShapeDtypeStruct, dtype=jnp.float32)
    local = functools.partial(pltpu.VMEM, dtype=jnp.float32)
    lon_count, lat_count = lax.axis_size("lon"), lax.axis_size("lat")
    lon, lat = lax.axis_index("lon"), lax.axis_index("lat")
    flags = jnp.stack([1 - lat % 2, 1 - lon % 2, (lat == lat_count - 1).astype(jnp.int32)])
    flags = flags.astype(jnp.int32)
    inputs = (
        direction,
        eof_basis,
        kappa_east,
        kappa_north,
        wet_mask,
        obs_base.reshape(1, -1),
        obs_frac.reshape(2, 1, -1),
        obs_rinv.reshape(levels, 1, -1),
    )
    own, far, close = pl.pallas_call(
        pack_tile,
        out_shape=(
            local((ROWS + 2, PAD, LANES)),
            local((HALO + 2, PAD, LANES)),
            local((HALO + 2, PAD, LANES)),
        ),
        in_specs=[pl.BlockSpec(memory_space=pltpu.HBM)] * len(inputs),
        out_specs=(VMEM,) * 3,
        scratch_shapes=[pltpu.VMEM(x.shape, x.dtype) for x in inputs]
        + [pltpu.SemaphoreType.DMA((len(inputs),))],
        compiler_params=grant(8),
    )(*(pltpu.with_memory_space_constraint(x, pltpu.HBM) for x in inputs))
    direction, residual = near(direction), near(residual)
    first, second = lat_pairs(lon_count, lat_count)
    dir_rows, res_rows = pl.pallas_call(
        by_rows,
        out_shape=(local((ROWS, PAD, LANES)),) * 2,
        in_specs=[VMEM] * 2,
        out_specs=(VMEM,) * 2,
        compiler_params=grant(8),
        cost_estimate=pl.CostEstimate(
            flops=0, bytes_accessed=1_300_000, transcendentals=0
        ),
    )(direction, residual)
    lat_b = lax.ppermute(far, ("lon", "lat"), second)
    lat_a = lax.ppermute(close, ("lon", "lat"), first)
    own, lat_a, lat_b = near(own), near(lat_a), near(lat_b)
    north_south, to_a, to_b = pl.pallas_call(
        pack_columns,
        out_shape=(local((2, HALO + 2, PAD, LANES)), local((8, PAD, LANES)), local((8, PAD, LANES))),
        in_specs=[SMEM] + [VMEM] * 3,
        out_specs=(VMEM,) * 3,
        compiler_params=grant(8),
    )(flags, own, lat_a, lat_b)
    first, second = lon_pairs(lon_count)
    lon_b = lax.ppermute(to_b, "lon", second)
    lon_a = lax.ppermute(to_a, "lon", first)
    image, part = pl.pallas_call(
        local_image,
        out_shape=(local(direction.shape), local((lon_count, LANES))),
        in_specs=[SMEM] + [VMEM] * 7,
        out_specs=(VMEM,) * 2,
        compiler_params=grant(28),
        scratch_shapes=[
            pltpu.VMEM((BAND, PAD, 2 * LANES), jnp.float32),
            pltpu.VMEM((BAND, PAD, 2 * LANES), jnp.float32),
            pltpu.VMEM((BAND, PAD, 2 * LANES), jnp.float32),
            pltpu.VMEM((5, BAND, 2 * LANES), jnp.float32),
            pltpu.VMEM((3, 3, PAD, 2 * LANES), jnp.float32),
        ],
    )(flags, own, near(north_south), near(lon_a), near(lon_b), near(dir_rows), near(res_rows), near(eof_basis.T))
    part = lax.all_to_all(part, "lon", 0, 0, tiled=True)
    part = jnp.broadcast_to(jnp.sum(part, axis=0, keepdims=True), (lat_count, LANES))
    part = lax.all_to_all(part, "lat", 0, 0, tiled=True)
    new_residual, new_direction, step_length = pl.pallas_call(
        finish,
        out_shape=(shape(direction.shape), shape(direction.shape), shape((1, 1))),
        in_specs=[VMEM] * 4,
        out_specs=(VMEM,) * 3,
        compiler_params=grant(8),
    )(near(part), near(image), residual, direction)
    return new_residual, new_direction, step_length.reshape(())


def solution(mesh):
    return jax.shard_map(
        per_device,
        mesh=mesh,
        in_specs=(
            P(None, "lat", "lon"),
            P(None, "lat", "lon"),
            P(),
            P("lat", "lon"),
            P("lat", "lon"),
            P("lat", "lon"),
            P("lat", "lon", None),
            P(None, "lat", "lon", None),
            P(None, "lat", "lon", None),
        ),
        out_specs=(P(None, "lat", "lon"), P(None, "lat", "lon"), P()),
        check_vma=False,
    )
```

```python
import functools

import jax
import jax.numpy as jnp
from jax import lax
from jax.experimental import pallas as pl
from jax.experimental.pallas import tpu as pltpu
from jax.sharding import PartitionSpec as P


HIGHEST = lax.Precision.HIGHEST
LANES = 128
ROWS = 8
PAD = 80
BAND = 3 * ROWS
HALO = 7
SLOTS = 12
SOUTH, OWN, NORTH = 0, 1, 2
EDGE, EDGE_ROW = 16, 4

SMEM = pl.BlockSpec(memory_space=pltpu.SMEM)
VMEM = pl.BlockSpec(memory_space=pltpu.VMEM)
HBM = pl.BlockSpec(memory_space=pltpu.HBM)
CHUNKS = 5


def grant(mebibytes):
    return pltpu.CompilerParams(vmem_limit_bytes=mebibytes << 20)


def near(x):
    return pltpu.with_memory_space_constraint(x, pltpu.VMEM)


def split(x):
    high = x.astype(jnp.bfloat16)
    return high, (x - high.astype(jnp.float32)).astype(jnp.bfloat16)


def dot3(left, right, dims):
    (lh, ll), (rh, rl) = left, right
    mul = functools.partial(
        lax.dot_general, dimension_numbers=(dims, ((), ())), preferred_element_type=jnp.float32
    )
    return mul(lh, rh) + (mul(lh, rl) + mul(ll, rh))


def pack_tile(*refs):
    count = (len(refs) - 4) // 2
    sources, held, sems = refs[:count], refs[count + 3 : -1], refs[-1]
    out_ref, far_ref, near_ref = refs[count : count + 3]
    copies = [
        pltpu.make_async_copy(source, target, sems.at[k])
        for k, (source, target) in enumerate(zip(sources, held))
    ]
    for copy in copies:
        copy.start()
    for copy in copies:
        copy.wait()
    dir_ref, eof_ref, ke_ref, kn_ref, wet_ref, base_ref, frac_ref, rinv_ref = held
    levels = dir_ref.shape[0]
    zeros = jnp.zeros((PAD - levels - 3, LANES), jnp.float32)
    eof = eof_ref[...]
    for row in range(ROWS):
        out_ref[row, :levels, :] = jnp.dot(
            eof, dir_ref[:, row, :], precision=HIGHEST, preferred_element_type=jnp.float32
        )
        out_ref[row, levels : levels + 1, :] = ke_ref[row : row + 1, :]
        out_ref[row, levels + 1 : levels + 2, :] = kn_ref[row : row + 1, :]
        out_ref[row, levels + 2 : levels + 3, :] = wet_ref[row : row + 1, :].astype(jnp.float32)
        out_ref[row, levels + 3 :, :] = zeros
    for half in range(2):
        cut = slice(half * LANES, (half + 1) * LANES)
        for level in range(levels):
            out_ref[ROWS + half, level : level + 1, :] = rinv_ref[level, :, cut]
        out_ref[ROWS + half, levels : levels + 1, :] = base_ref[:, cut].astype(jnp.float32)
        out_ref[ROWS + half, levels + 1 : levels + 2, :] = frac_ref[0, :, cut]
        out_ref[ROWS + half, levels + 2 : levels + 3, :] = frac_ref[1, :, cut]
        out_ref[ROWS + half, levels + 3 :, :] = zeros
        far_ref[HALO + half] = out_ref[ROWS + half]
        near_ref[HALO + half] = out_ref[ROWS + half]
    northern = lax.axis_index("lat") % 2 == 1
    for row in range(HALO):
        low, high = out_ref[row], out_ref[row + 1]
        far_ref[row] = jnp.where(northern, high, low)
        near_ref[row] = jnp.where(northern, low, high)


def by_rows(dir_ref, res_ref, dir_rows_ref, res_rows_ref):
    for source, target in ((dir_ref, dir_rows_ref), (res_ref, res_rows_ref)):
        for row in range(ROWS):
            target[row, : source.shape[0], :] = source[:, row, :]


def row_tile(own_ref, ns_ref, index):
    if index in (0, BAND - 1):
        return None
    if index < ROWS:
        return ns_ref[1, index - 1]
    return own_ref[index - ROWS] if index < 2 * ROWS else ns_ref[0, index - 2 * ROWS]


def pack_columns(flags, own_ref, ra_ref, rb_ref, ns_ref, pa_ref, pb_ref):
    lat_even, lon_even, is_top = flags[0] == 1, flags[1] == 1, flags[2] == 1

    @pl.when(lat_even)
    def _():
        ns_ref[0] = ra_ref[...]
        ns_ref[1] = rb_ref[...]

    @pl.when(jnp.logical_not(lat_even))
    def _():
        ns_ref[0] = rb_ref[...]
        ns_ref[1] = ra_ref[...]

    @pl.when(is_top)
    def _():
        first = lax.broadcasted_iota(jnp.int32, (LANES, LANES), 0)
        second = lax.broadcasted_iota(jnp.int32, (LANES, LANES), 1)
        flip = jnp.where(first + second == LANES - 1, 1.0, 0.0).astype(jnp.float32)
        for row in range(HALO):
            ns_ref[0, row] = jnp.dot(
                rb_ref[HALO - 1 - row], flip, precision=HIGHEST, preferred_element_type=jnp.float32
            )

    lane = lax.broadcasted_iota(jnp.int32, (PAD, LANES), 1)
    for group in range(2):
        west = jnp.zeros((PAD, LANES), jnp.float32)
        east = jnp.zeros((PAD, LANES), jnp.float32)
        for slot in range(SLOTS):
            tile = row_tile(own_ref, ns_ref, group * SLOTS + slot)
            if tile is None:
                continue
            start = HALO * slot
            here = (lane >= start) & (lane < start + HALO)
            west = jnp.where(here, pltpu.roll(tile, start, 1) if start else tile, west)
            east = jnp.where(here, pltpu.roll(tile, (start + HALO) % LANES, 1), east)
        pa_ref[group] = jnp.where(lon_even, east, west)
        pb_ref[group] = jnp.where(lon_even, west, east)
    for half in range(2):
        for ref in (pa_ref, pb_ref):
            ref[2 + 2 * SOUTH + half] = ns_ref[1, HALO + half]
            ref[2 + 2 * OWN + half] = own_ref[ROWS + half]
            ref[2 + 2 * NORTH + half] = ns_ref[0, HALO + half]


def diffuse_row(src, dst, coef, index):
    centre = src[index]
    width = centre.shape[1]
    wide = lambda k: jnp.broadcast_to(coef[k, pl.ds(index, 1), :], centre.shape)
    out = centre * wide(0)
    out = out + wide(1) * pltpu.roll(centre, width - 1, 1)
    out = out + wide(2) * pltpu.roll(centre, 1, 1)
    out = out + wide(3) * src[index + 1]
    out = out + wide(4) * src[index - 1]
    dst[index] = out


def diffuse_own(src, dst, coef, index):
    own, beyond = src[index, :, :LANES], src[index, :, LANES:]
    lane = lax.broadcasted_iota(jnp.int32, own.shape, 1)
    wide = lambda k: jnp.broadcast_to(coef[k, pl.ds(index, 1), :LANES], own.shape)
    out = own * wide(0)
    out = out + wide(1) * pltpu.roll(jnp.where(lane == 0, beyond, own), LANES - 1, 1)
    out = out + wide(2) * pltpu.roll(jnp.where(lane == LANES - 1, beyond, own), 1, 1)
    out = out + wide(3) * src[index + 1, :, :LANES]
    out = out + wide(4) * src[index - 1, :, :LANES]
    dst[index, :, :LANES] = out


def diffuse_all(one, two, coef, low, high, last=diffuse_row):
    for src, dst, trim, step in (
        (one, two, 0, diffuse_row),
        (two, one, 1, diffuse_row),
        (one, two, 2, last),
    ):
        for index in range(low + trim, high - trim):
            step(src, dst, coef, index)


def local_image(
    flags,
    own_ref,
    ns_ref,
    qa_ref,
    qb_ref,
    dir_ref,
    res_ref,
    eoft_ref,
    img_ref,
    part_ref,
    field,
    other,
    adj,
    coef,
    obs,
):
    lon_even, is_top = flags[1] == 1, flags[2] == 1
    levels = img_ref.shape[0]
    width = 2 * LANES
    lane = lax.broadcasted_iota(jnp.int32, (PAD, LANES), 1)
    for group in range(2):
        first, second = qa_ref[group], qb_ref[group]
        east = jnp.where(lon_even, first, second)
        west = jnp.where(lon_even, second, first)
        for slot in range(SLOTS):
            index = group * SLOTS + slot
            tile = row_tile(own_ref, ns_ref, index)
            if tile is None:
                field[index] = jnp.zeros((PAD, width), jnp.float32)
                continue
            start = HALO * slot
            from_east = pltpu.roll(east, (LANES - start) % LANES, 1) if start else east
            from_west = pltpu.roll(west, (LANES - HALO - start) % LANES, 1)
            field[index, :, :LANES] = tile
            field[index, :, LANES:] = jnp.where(
                lane < HALO, from_east, jnp.where(lane >= LANES - HALO, from_west, 0.0)
            )

    ke, kn, wet = field[:, levels, :], field[:, levels + 1, :], field[:, levels + 2, :]
    row = lax.broadcasted_iota(jnp.int32, (BAND, width), 0)
    up = lambda x: jnp.concatenate([x[1:], x[:1]], 0)
    down = lambda x: jnp.concatenate([x[-1:], x[:-1]], 0)
    right = lambda x: pltpu.roll(x, width - 1, 1)
    left = lambda x: pltpu.roll(x, 1, 1)
    seam = 2 * ROWS - 1
    top = jnp.where(is_top, 1, 0)
    ke = jnp.where((row > seam) & (top == 1), right(ke), ke)
    kn_up = up(kn)
    kn = jnp.where(
        top == 1, jnp.where(row > seam, kn_up, jnp.where(row == seam, 0.5 * (kn + kn_up), kn)), kn
    )
    east_face = ke * wet * right(wet)
    north_face = kn * wet * up(wet)
    west_face, south_face = left(east_face), down(north_face)
    coef[0] = 1.0 - east_face - west_face - north_face - south_face
    coef[1] = east_face
    coef[2] = west_face
    coef[3] = north_face
    coef[4] = south_face

    diffuse_all(field, other, coef, 2, BAND - 2)
    physical = other

    for band in range(3):
        for half in range(2):
            cut = slice(half * LANES, (half + 1) * LANES)
            slot = 2 + 2 * band + half
            first, second = qa_ref[slot], qb_ref[slot]
            mid = (ns_ref[1, HALO + half], own_ref[ROWS + half], ns_ref[0, HALO + half])[band]
            obs[0, band, :, cut] = jnp.where(lon_even, second, first)
            obs[1, band, :, cut] = jnp.where(lon_even, first, second)
            obs[2, band, :, cut] = mid
    adj[...] = jnp.zeros(adj.shape, jnp.float32)
    cells = lax.broadcasted_iota(jnp.int32, (width, width), 0)
    keep = lax.broadcasted_iota(jnp.int32, (PAD, width), 0) < levels

    def places(side, band):
        base = obs[side, band, levels : levels + 1, :].astype(jnp.int32)
        p = obs[side, band, levels + 1 : levels + 2, :]
        q = obs[side, band, levels + 2 : levels + 3, :]
        j, i = base >> 7, base & (LANES - 1)
        turned = (top if band == NORTH else 0 * top) == 1
        rows = jnp.where(turned, 22 - j, j + ROWS * band)
        cols = jnp.where(turned, 126 - i, i)
        a0, a1 = jnp.where(turned, p, 1.0 - p), jnp.where(turned, 1.0 - p, p)
        b0, b1 = jnp.where(turned, q, 1.0 - q), jnp.where(turned, 1.0 - q, q)
        return rows, cols, a0, a1, b0, b1

    def weigh(side, band, profile):
        return jnp.where(keep, obs[side, band] * profile, 0.0)

    packed = [jnp.zeros((PAD, LANES), jnp.float32)] * 2
    for k in range(EDGE):
        own, beyond = physical[EDGE_ROW + k, :, :LANES], physical[EDGE_ROW + k, :, LANES:]
        west = pltpu.roll(jnp.where(lane < LANES // 2, own, beyond), (EDGE * k + 4) % LANES, 1)
        east = pltpu.roll(jnp.where(lane < LANES // 2, beyond, own), (EDGE * k + 12) % LANES, 1)
        half, first = k // 8, EDGE * (k % 8)
        packed[half] = jnp.where(
            (lane >= first) & (lane < first + 8),
            west,
            jnp.where((lane >= first + 8) & (lane < first + EDGE), east, packed[half]),
        )
    packed = jnp.concatenate(packed, 1)
    packed = split(packed)
    edge_col = lax.broadcasted_iota(jnp.int32, (EDGE, width), 0)

    def beside(step, total):
        side, band = step & 1, step >> 1
        rows, cols, a0, a1, b0, b1 = places(side, band)
        rows = rows - EDGE_ROW
        cols = cols + jnp.where(side == 0, -124, 12)
        col_weight = jnp.where(edge_col == cols, b0, jnp.where(edge_col == cols + 1, b1, 0.0))
        rows, a0, a1 = (jnp.broadcast_to(x, (8, width)) for x in (rows, a0, a1))
        parts = []
        for k in range(EDGE):
            row_weight = jnp.where(rows == k, a0, jnp.where(rows == k - 1, a1, 0.0))
            parts += [row_weight * col_weight[:8], row_weight * col_weight[8:]]
        rhs = split(jnp.concatenate(parts, 0))
        weighted = weigh(side, band, dot3(packed, rhs, ((1,), (0,))))
        return total + dot3(split(weighted), rhs, ((1,), (1,)))

    total = jnp.zeros((PAD, width), jnp.float32)
    for step in range(6):
        total = beside(step, total)
    for k in range(1, EDGE - 1):
        half = k // 8
        here = total[:, half * LANES : (half + 1) * LANES]
        west = pltpu.roll(here, (2 * LANES - EDGE * (k % 8) - 4) % LANES, 1)
        east = pltpu.roll(here, (2 * LANES - EDGE * (k % 8) - 12) % LANES, 1)
        low, high = lane < 4, lane >= LANES - 4
        adj[EDGE_ROW + k, :, :LANES] = jnp.where(low, west, jnp.where(high, east, 0.0))
        adj[EDGE_ROW + k, :, LANES:] = jnp.where(low, east, jnp.where(high, west, 0.0))

    for band, (begin, stop, lo, hi) in enumerate(((4, 9, 5, 9), (8, 17, 8, 17), (16, 20, 16, 19))):
        lhs = split(physical[begin:stop].reshape((stop - begin) * PAD, width))
        rows, cols, a0, a1, b0, b1 = places(2, band)
        lane0 = cols & (width - 1)
        lane1 = (cols + 1) & (width - 1)
        rhs = split(jnp.where(cells == lane0, b0, jnp.where(cells == lane1, b1, 0.0)))
        taken = dot3(lhs, rhs, ((1,), (0,)))
        row_weight = [
            jnp.where(rows == r, a0, jnp.where(rows == r - 1, a1, 0.0)) for r in range(begin, stop)
        ]
        profile = jnp.zeros((PAD, width), jnp.float32)
        for k in range(stop - begin):
            profile = profile + row_weight[k] * taken[k * PAD : (k + 1) * PAD]
        weighted = weigh(2, band, profile)
        spread = jnp.concatenate([row_weight[r - begin] * weighted for r in range(lo, hi)], 0)
        added = dot3(split(spread), rhs, ((1,), (1,)))
        adj[lo:hi] += added.reshape(hi - lo, PAD, width)

    diffuse_all(adj, other, coef, 6, BAND - 6, diffuse_own)

    eoft = split(eoft_ref[...])
    rr = dim = rim = imim = jnp.zeros((levels, LANES), jnp.float32)
    for r in range(ROWS):
        back = dot3(eoft, split(other[ROWS + r, :levels, :LANES]), ((1,), (0,)))
        d, res = dir_ref[r, :levels, :], res_ref[r, :levels, :]
        image = d + back
        img_ref[:, r, :] = image
        rr, dim, rim, imim = rr + res * res, dim + d * image, rim + res * image, imim + image * image
    lane = lax.broadcasted_iota(jnp.int32, part_ref.shape, 1)
    out = jnp.zeros(part_ref.shape, jnp.float32)
    for k, value in enumerate((rr, dim, rim, imim)):
        out = jnp.where(lane == k, jnp.sum(value), out)
    part_ref[...] = out


def finish(
    part_ref, img_ref, res_ref, dir_ref, new_res_ref, new_dir_ref, step_ref, res_buf, dir_buf, sems
):
    total = jnp.sum(part_ref[...], axis=0, keepdims=True)
    lane = lax.broadcasted_iota(jnp.int32, total.shape, 1)
    rr, dim, rim, imim = (
        jnp.sum(jnp.where(lane == k, total, 0.0), axis=1, keepdims=True) for k in range(4)
    )
    step = rr / dim
    new_norm = rr + step * (step * imim - 2.0 * rim)
    beta = new_norm / rr
    step_ref[...] = step
    chunk = res_buf.shape[0] // CHUNKS
    copies = []
    for k in range(CHUNKS):
        cut = slice(k * chunk, (k + 1) * chunk)
        new_res = res_ref[cut] - step[None] * img_ref[cut]
        res_buf[cut] = new_res
        dir_buf[cut] = new_res + beta[None] * dir_ref[cut]
        copies += [
            pltpu.make_async_copy(res_buf.at[cut], new_res_ref.at[cut], sems.at[2 * k]),
            pltpu.make_async_copy(dir_buf.at[cut], new_dir_ref.at[cut], sems.at[2 * k + 1]),
        ]
        copies[-2].start()
        copies[-1].start()
    for copy in copies:
        copy.wait()


def lat_pairs(lon_count, lat_count):
    index = lambda lon, lat: lon * lat_count + lat
    first, second = [], []
    for lon in range(lon_count):
        for lat in range(lat_count):
            first.append((index(lon, lat), index(lon, lat ^ 1)))
            other = lat + 1 if lat % 2 else lat - 1
            if other == lat_count:
                second.append((index(lon, lat), index(lon_count - 1 - lon, lat)))
            elif other >= 0:
                second.append((index(lon, lat), index(lon, other)))
    return first, second


def lon_pairs(lon_count):
    first = [(lon, lon ^ 1) for lon in range(lon_count)]
    second = [(lon, (lon + 1 if lon % 2 else lon - 1) % lon_count) for lon in range(lon_count)]
    return first, second


def per_device(
    direction, residual, eof_basis, kappa_east, kappa_north, wet_mask, obs_base, obs_frac, obs_rinv
):
    levels = direction.shape[0]
    shape = functools.partial(jax.ShapeDtypeStruct, dtype=jnp.float32)
    local = functools.partial(pltpu.VMEM, dtype=jnp.float32)
    lon_count, lat_count = lax.axis_size("lon"), lax.axis_size("lat")
    lon, lat = lax.axis_index("lon"), lax.axis_index("lat")
    flags = jnp.stack([1 - lat % 2, 1 - lon % 2, (lat == lat_count - 1).astype(jnp.int32)])
    flags = flags.astype(jnp.int32)
    inputs = (
        direction,
        eof_basis,
        kappa_east,
        kappa_north,
        wet_mask,
        obs_base.reshape(1, -1),
        obs_frac.reshape(2, 1, -1),
        obs_rinv.reshape(levels, 1, -1),
    )
    own, far, close = pl.pallas_call(
        pack_tile,
        out_shape=(
            local((ROWS + 2, PAD, LANES)),
            local((HALO + 2, PAD, LANES)),
            local((HALO + 2, PAD, LANES)),
        ),
        in_specs=[pl.BlockSpec(memory_space=pltpu.HBM)] * len(inputs),
        out_specs=(VMEM,) * 3,
        scratch_shapes=[pltpu.VMEM(x.shape, x.dtype) for x in inputs]
        + [pltpu.SemaphoreType.DMA((len(inputs),))],
        compiler_params=grant(8),
    )(*(pltpu.with_memory_space_constraint(x, pltpu.HBM) for x in inputs))
    direction, residual = near(direction), near(residual)
    first, second = lat_pairs(lon_count, lat_count)
    dir_rows, res_rows = pl.pallas_call(
        by_rows,
        out_shape=(local((ROWS, PAD, LANES)),) * 2,
        in_specs=[VMEM] * 2,
        out_specs=(VMEM,) * 2,
        compiler_params=grant(8),
        cost_estimate=pl.CostEstimate(
            flops=0, bytes_accessed=1_300_000, transcendentals=0
        ),
    )(direction, residual)
    lat_b = lax.ppermute(far, ("lon", "lat"), second)
    lat_a = lax.ppermute(close, ("lon", "lat"), first)
    own, lat_a, lat_b = near(own), near(lat_a), near(lat_b)
    north_south, to_a, to_b = pl.pallas_call(
        pack_columns,
        out_shape=(local((2, HALO + 2, PAD, LANES)), local((8, PAD, LANES)), local((8, PAD, LANES))),
        in_specs=[SMEM] + [VMEM] * 3,
        out_specs=(VMEM,) * 3,
        compiler_params=grant(8),
    )(flags, own, lat_a, lat_b)
    first, second = lon_pairs(lon_count)
    lon_b = lax.ppermute(to_b, "lon", second)
    lon_a = lax.ppermute(to_a, "lon", first)
    image, part = pl.pallas_call(
        local_image,
        out_shape=(local(direction.shape), local((lon_count, LANES))),
        in_specs=[SMEM] + [VMEM] * 7,
        out_specs=(VMEM,) * 2,
        compiler_params=grant(28),
        scratch_shapes=[
            pltpu.VMEM((BAND, PAD, 2 * LANES), jnp.float32),
            pltpu.VMEM((BAND, PAD, 2 * LANES), jnp.float32),
            pltpu.VMEM((BAND, PAD, 2 * LANES), jnp.float32),
            pltpu.VMEM((5, BAND, 2 * LANES), jnp.float32),
            pltpu.VMEM((3, 3, PAD, 2 * LANES), jnp.float32),
        ],
    )(flags, own, near(north_south), near(lon_a), near(lon_b), near(dir_rows), near(res_rows), near(eof_basis.T))
    part = lax.all_to_all(part, "lon", 0, 0, tiled=True)
    part = jnp.broadcast_to(jnp.sum(part, axis=0, keepdims=True), (lat_count, LANES))
    part = lax.all_to_all(part, "lat", 0, 0, tiled=True)
    new_residual, new_direction, step_length = pl.pallas_call(
        finish,
        out_shape=(shape(direction.shape), shape(direction.shape), shape((1, 1))),
        in_specs=[VMEM] * 4,
        out_specs=(HBM, HBM, VMEM),
        scratch_shapes=[
            pltpu.VMEM(direction.shape, jnp.float32),
            pltpu.VMEM(direction.shape, jnp.float32),
            pltpu.SemaphoreType.DMA((2 * CHUNKS,)),
        ],
        compiler_params=grant(8),
    )(near(part), near(image), residual, direction)
    return new_residual, new_direction, step_length.reshape(())


def solution(mesh):
    return jax.shard_map(
        per_device,
        mesh=mesh,
        in_specs=(
            P(None, "lat", "lon"),
            P(None, "lat", "lon"),
            P(),
            P("lat", "lon"),
            P("lat", "lon"),
            P("lat", "lon"),
            P("lat", "lon", None),
            P(None, "lat", "lon", None),
            P(None, "lat", "lon", None),
        ),
        out_specs=(P(None, "lat", "lon"), P(None, "lat", "lon"), P()),
        check_vma=False,
    )
```
